128 devices in a mesh: row: 8 (over y, x_hi), col: 16 (over z, x_lo, core).
Axes of the slice: x: 4 (x_hi: 2, x_lo: 2; x = x_hi * 2 + x_lo), y: 4, z: 4, core: 2. Of those that a mesh axis runs over, the one named last changes fastest.
Arguments:
- a_blocks: bfloat16 [16, 8, 16, 32, 128], P('col', 'row'), may hold values from -1 to 1
- a_scale: float32 [16, 8, 16, 4], P('col', 'row'), may hold values from 0.25 to 4
- a_cols: int32 [16, 8, 16, 4], P('col', 'row'), may hold values from 0 to 511, as said below
- b_blocks: bfloat16 [16, 8, 512, 32, 128], P('col', 'row'), may hold values from -1 to 1
- b_scale: float32 [16, 8, 512, 4], P('col', 'row'), may hold values from 0.25 to 4
- b_cols: int32 [16, 8, 512, 4], P('col', 'row'), may hold values from 0 to 511, as said below
Outputs:
- product: bfloat16 [16, 8, 8, 32, 16384], P('col', 'row')
The draws below stay inside these ranges and needn't reach their ends.
Inputs may be any that keep to these rules, and one draw needn't show every extreme that they name: `a_cols`: the 4 columns of each block row are distinct. `b_cols`: the 4 columns of each block row are distinct.
All inputs are finite; a program needn't handle non-finite values.
Results may differ from the reference program's by a relative error of at most 0.0034.
Values may be sent and summed in bfloat16 or wider, within the bound.
A program may use at most 192 MiB of HBM per device.

```python
import math
import jax
import jax.numpy as jnp
from jax import lax

BS = 32
ROWS = 16
JW = 512
RA = 4
RB = 4
KW = 512
N_ROW = 8
N_COL = 16


def distinct_columns(key, count, limit, picks):
    scores = jax.random.randint(key, (count, limit), 0, 1 << 20) * limit + jnp.arange(limit, dtype=jnp.int32)
    return lax.top_k(scores, picks)[1].astype(jnp.int32)


def draw_a_cols(key, part):
    picked = distinct_columns(jax.random.fold_in(key, 11), N_COL * N_ROW * ROWS, KW, RA)
    return picked.reshape(N_COL, N_ROW, ROWS, RA)


def draw_b_cols(key, part):
    picked = distinct_columns(jax.random.fold_in(key, 23), N_COL * N_ROW * KW, JW, RB)
    return picked.reshape(N_COL, N_ROW, KW, RB)


def steps_of(key, shape, shards, least, largest):
    def one(position, shards_of):
        draws = jax.random.uniform(jax.random.fold_in(jax.random.fold_in(key, 6), position), (shards_of,), jnp.float32, least / len(shards), largest / len(shards))
        return jnp.repeat(jnp.exp(draws), shape[position] // shards_of).reshape((-1,) + (1,) * (len(shape) - position - 1))

    loudness = one(*shards[0])
    for cut in shards[1:]:
        loudness = loudness * one(*cut)
    return loudness


def gaussian(stream_key, shape, width, most, pieces=(), kind=jnp.bfloat16):
    drawn = jax.random.normal(stream_key, shape, jnp.float32) * width
    if len(pieces) > 0:
        drawn = steps_of(stream_key, shape, pieces, -0.22, 0.18) * drawn
    return jnp.clip(drawn, min=-most, max=most).astype(kind)


def setup_inputs(seed: int = 0) -> dict:
    streams_of = jax.random.split(jax.random.key(seed), 7)
    return {
        "a_blocks": gaussian(streams_of[0], (N_COL, N_ROW, ROWS, BS, RA * BS), 0.125, 1.0, ((0, 16), (1, 8))),
        "a_scale": jnp.clip(jnp.exp(math.log(4.0) - 2.7725887 * jax.random.uniform(streams_of[1], (N_COL, N_ROW, ROWS, RA), jnp.float32) ** steps_of(streams_of[1], (N_COL, N_ROW, ROWS, RA), ((0, 16), (1, 8)), -0.2, 0.2)), 0.25, 4.0),
        "a_cols": draw_a_cols(jax.random.fold_in(streams_of[6], 71), 0),
        "b_blocks": gaussian(streams_of[3], (N_COL, N_ROW, KW, BS, RB * BS), 0.125, 1.0, ((0, 16), (1, 8))),
        "b_scale": jnp.clip(jnp.exp(math.log(4.0) - 2.7725887 * jax.random.uniform(streams_of[4], (N_COL, N_ROW, KW, RB), jnp.float32) ** steps_of(streams_of[4], (N_COL, N_ROW, KW, RB), ((0, 16), (1, 8)), -0.2, 0.2)), 0.25, 4.0),
        "b_cols": draw_b_cols(jax.random.fold_in(streams_of[6], 71), 0),
    }


def block_sum(total, a_part, a_scl, a_idx, b_part, b_scl, b_idx):
    nrows, bsize, _ = a_part.shape
    slots_a = a_scl.shape[1]
    slots_b = b_scl.shape[1]
    left = a_part.reshape(nrows, bsize, slots_a, bsize).astype(jnp.float32)
    right = jnp.take(b_part, a_idx, axis=0).astype(jnp.float32)
    right_scl = jnp.take(b_scl, a_idx, axis=0)
    right_idx = jnp.take(b_idx, a_idx, axis=0)
    prods = lax.dot_general(left, right, (((3,), (2,)), ((0, 2), (0, 1))), precision=lax.Precision.HIGHEST, preferred_element_type=jnp.float32)
    prods = prods.reshape(nrows, slots_a, bsize, slots_b, bsize)
    prods = jnp.transpose(prods, (0, 1, 3, 2, 4))
    scaled = prods * (a_scl[:, :, None] * right_scl)[..., None, None]
    scaled = scaled.reshape(nrows, slots_a, slots_b, bsize * bsize)
    row_ids = jnp.broadcast_to(jnp.arange(nrows, dtype=jnp.int32)[:, None, None], right_idx.shape)
    return total.at[row_ids, right_idx].add(scaled)


def reference(a_blocks, a_scale, a_cols, b_blocks, b_scale, b_cols):
    panels = N_ROW

    def one_panel(index):
        owner = index // panels
        target = index % panels

        def partial_value(half):
            def tick(inner, total):
                a_at = (inner - owner) % panels
                b_at = 2 * ((inner - target) % panels) + half
                a_row = 2 * owner + half
                return block_sum(total, a_blocks[a_row, a_at], a_scale[a_row, a_at], a_cols[a_row, a_at], b_blocks[b_at, target], b_scale[b_at, target], b_cols[b_at, target])

            start = jnp.zeros((ROWS, JW, BS * BS), jnp.float32)
            summed = lax.fori_loop(0, panels, tick, start)
            return lax.optimization_barrier(summed.astype(jnp.bfloat16)).astype(jnp.float32)

        whole = (partial_value(0) + partial_value(1)).astype(jnp.bfloat16)
        whole = whole.reshape(ROWS, JW, BS, BS)
        return jnp.transpose(whole, (0, 2, 1, 3)).reshape(ROWS, BS, JW * BS)

    every = lax.map(one_panel, jnp.arange(panels * panels, dtype=jnp.int32))
    every = every.reshape(panels, panels, 2, ROWS // 2, BS, JW * BS)
    every = jnp.transpose(every, (0, 2, 1, 3, 4, 5))
    return every.reshape(2 * panels, panels, ROWS // 2, BS, JW * BS)
```

```python
import jax
import jax.numpy as jnp
from jax import lax
from jax.experimental import pallas as pl
from jax.experimental.pallas import tpu as pltpu
from jax.sharding import PartitionSpec as P

MESH = pl.DeviceIdType.MESH
F32, BF16, I32 = jnp.float32, jnp.bfloat16, jnp.int32

OFFSETS = ((1, 0), (0, 1), (3, 0), (1, 1), (2, 0), (3, 1), (2, 1), (0, 0))
HOPS = (1, 3, 2)


def lane_groups(v, group):
    low, high = group % 2 == 0, group < 2
    t = [None] * 4
    for i in (0, 2):
        t[i] = jnp.where(low, v[i], pltpu.roll(v[i + 1], 32, 1))
        t[i + 1] = jnp.where(low, pltpu.roll(v[i], 96, 1), v[i + 1])
    w = [None] * 4
    for i in (0, 1):
        w[i] = jnp.where(high, t[i], pltpu.roll(t[i + 2], 64, 1))
        w[i + 2] = jnp.where(high, pltpu.roll(t[i], 64, 1), t[i + 2])
    return w


def exchange_kernel(
    cols_ref, scale_ref, a_ref, b_ref, bs_ref, bc_ref,
    brecv, arecv, ocols, oscale,
    b_vm, bsend, idx_s, idx_r, as_s, as_r, idx_sm, as_sm, table, msend, mrecv,
    local_sem, idx_ss, idx_rs, as_ss, as_rs, b_ss, b_rs, m_ss, m_rs, a_ss, a_rs,
):
    c, r = lax.axis_index("col"), lax.axis_index("row")
    s, q = c // 2, c % 2
    z, xl, y, xh = s // 2, s % 2, r // 2, r % 2
    k = (s + r) % 8
    rx = y * 2 + (1 - xh)
    kx = (s + rx) % 8

    def dev(s_, q_, r_):
        return {"row": r_, "col": 2 * s_ + q_}

    def chip(d):
        dz, dx = OFFSETS[d]
        return ((z + dz) % 4) * 2 + (1 - xl if dx else xl)

    def chip_behind(d):
        dz, dx = OFFSETS[d]
        return ((z + 4 - dz) % 4) * 2 + (1 - xl if dx else xl)

    def row_at(dy):
        return ((y + dy) % 4) * 2 + xh

    def send(src, dst, ssem, rsem, target):
        return pltpu.make_async_remote_copy(
            src_ref=src, dst_ref=dst, send_sem=ssem, recv_sem=rsem, device_id=target, device_id_type=MESH
        )

    load_b = pltpu.make_async_copy(b_ref, b_vm, local_sem.at[0])
    load_b.start()
    idx_s[...] = jnp.zeros_like(idx_s)
    as_s[...] = jnp.zeros_like(as_s)
    idx_s[0:4, 0:16] = cols_ref[...]
    as_s[0:4, 0:16] = scale_ref[...]

    barrier = pltpu.get_barrier_semaphore()
    peers = []
    for d in range(8):
        for p in range(2):
            if d < 7:
                peers.append(dev(chip(d), p, r))
    peers.append(dev(s, 1 - q, r))
    for p in range(2):
        peers.append(dev(s, p, rx))
    for dy in HOPS:
        peers.append(dev(s, q, row_at(dy)))
    for e in range(1, 8):
        peers.append(dev((s + 8 - e) % 8, q, (r + e) % 8))
    for peer in peers:
        pl.semaphore_signal(barrier, inc=1, device_id=peer, device_id_type=MESH)
    pl.semaphore_wait(barrier, len(peers))

    idx_sends = []
    for e in range(1, 8):
        to = dev((s + 8 - e) % 8, q, (r + e) % 8)
        idx_sends.append(send(idx_s, idx_r.at[s], idx_ss.at[e - 1], idx_rs.at[s], to))
        idx_sends.append(send(as_s, as_r.at[s], as_ss.at[e - 1], as_rs.at[s], to))
    for copy in idx_sends:
        copy.start()

    own_half = a_ref.at[pl.ds(pl.multiple_of(q * 8, 8), 8)]
    other_half = a_ref.at[pl.ds(pl.multiple_of((1 - q) * 8, 8), 8)]
    a_sends = [send(a_ref.at[pl.ds(p * 8, 8)], arecv.at[k, q], a_ss.at[1 + p], a_rs.at[1 + q], dev(s, p, rx)) for p in range(2)]
    a_sends.append(send(other_half, arecv.at[k, q], a_ss.at[0], a_rs.at[0], dev(s, 1 - q, r)))
    for copy in a_sends:
        copy.start()
    own_a = pltpu.make_async_copy(own_half, arecv.at[k, q], local_sem.at[1])
    own_a.start()

    idx_r[s] = idx_s[...]
    as_r[s] = as_s[...]
    for g in range(4):
        lanes = pl.ds(g * 128, 128)
        eight = jnp.concatenate([bs_ref[:, lanes], bc_ref[:, lanes].astype(F32)], axis=0)
        table[pl.ds(g * 128, 128), :] = jnp.transpose(jnp.concatenate([eight] * 16, axis=0))

    for e in range(1, 8):
        sb, rb = (s + e) % 8, (r + 8 - e) % 8
        send(idx_s, idx_r.at[sb], idx_ss.at[e - 1], idx_rs.at[sb], dev(sb, q, rb)).wait_recv()
        send(as_s, as_r.at[sb], as_ss.at[e - 1], as_rs.at[sb], dev(sb, q, rb)).wait_recv()
    to_smem = pltpu.make_async_copy(idx_r, idx_sm, local_sem.at[2])
    to_smem.start()
    to_smem2 = pltpu.make_async_copy(as_r, as_sm, local_sem.at[3])
    to_smem2.start()
    to_smem.wait()
    to_smem2.wait()
    load_b.wait()

    b_sends = []
    pending = []
    for d in range(8):
        sd = chip(d)

        def gather(i, _):
            for m in range(4):
                bsend[d, i // 8, (i % 8) * 4 + m] = b_vm[idx_sm[sd, m, i]]
            return _

        lax.fori_loop(0, 16, gather, 0)
        for copy in pending:
            copy.start()
        b_sends += pending
        pending = []
        if d < 7:
            for p in range(2):
                pending.append(send(bsend.at[d, p], brecv.at[k, q], b_ss.at[2 * d + p], b_rs.at[k, q], dev(sd, p, r)))
    own_b = pltpu.make_async_copy(bsend.at[7, q], brecv.at[k, q], local_sem.at[4])
    to_core = send(bsend.at[7, 1 - q], brecv.at[k, q], b_ss.at[14], b_rs.at[k, q], dev(s, 1 - q, r))

    own_a.wait()
    send(other_half, arecv.at[k, 1 - q], a_ss.at[0], a_rs.at[0], dev(s, 1 - q, r)).wait_recv()
    for p in range(2):
        send(own_half, arecv.at[kx, p], a_ss.at[1 + p], a_rs.at[1 + p], dev(s, p, rx)).wait_recv()
    own_b.start()
    to_core.start()
    for h, dy in enumerate(HOPS):
        for j, slot in enumerate((k, kx)):
            n = 3 + 2 * h + j
            copy = send(arecv.at[slot], arecv.at[slot], a_ss.at[n], a_rs.at[n], dev(s, q, row_at(dy)))
            copy.start()
            a_sends.append(copy)

    lane = lax.broadcasted_iota(I32, (1, 128), 1)
    part, place = lane % 8, lane // 8
    m_sends = []
    for d in range(8):
        sd = chip(d)

        def metas(n, _):
            row = jnp.zeros((1, 128), F32)
            for w in range(16):
                i, m = n * 4 + w // 4, w % 4
                factor = jnp.where(part < 4, as_sm[sd, m, i], 1.0)
                row = jnp.where(place == w, table[pl.ds(idx_sm[sd, m, i], 1), :] * factor, row)
            msend[d, n // 2, pl.ds(n % 2, 1), :] = row
            return _

        lax.fori_loop(0, 4, metas, 0)
    for d in range(7):
        for p in range(2):
            copy = send(msend.at[d, p], mrecv.at[k, q], m_ss.at[2 * d + p], m_rs.at[k, q], dev(chip(d), p, r))
            copy.start()
            m_sends.append(copy)
    copy = send(msend.at[7, 1 - q], mrecv.at[k, q], m_ss.at[14], m_rs.at[k, q], dev(s, 1 - q, r))
    copy.start()
    m_sends.append(copy)
    mrecv[k, q] = msend[7, q]

    own_b.wait()
    for d in range(8):
        sb = chip_behind(d)
        kb = (sb + r) % 8
        for p in range(2):
            if d < 7:
                send(bsend.at[d, p], brecv.at[kb, p], b_ss.at[2 * d + p], b_rs.at[kb, p], dev(sb, p, r)).wait_recv()
                send(msend.at[d, p], mrecv.at[kb, p], m_ss.at[2 * d + p], m_rs.at[kb, p], dev(sb, p, r)).wait_recv()
    send(bsend.at[7, q], brecv.at[k, 1 - q], b_ss.at[14], b_rs.at[k, 1 - q], dev(s, 1 - q, r)).wait_recv()
    send(msend.at[7, q], mrecv.at[k, 1 - q], m_ss.at[14], m_rs.at[k, 1 - q], dev(s, 1 - q, r)).wait_recv()
    for h, dy in enumerate(HOPS):
        rb = row_at(4 - dy)
        for j, rr in enumerate((rb, (rb // 2) * 2 + (1 - xh))):
            slot = (s + rr) % 8
            n = 3 + 2 * h + j
            send(arecv.at[slot], arecv.at[slot], a_ss.at[n], a_rs.at[n], dev(s, q, rb)).wait_recv()
    for kk in range(8):
        for qq in range(2):
            two = mrecv[kk, qq, 0:2, :]
            n = (kk * 2 + qq) * 2
            ocols[n:n + 2, :] = two.astype(I32)
            oscale[n:n + 2, :] = two
    for copy in idx_sends + a_sends + b_sends + [to_core] + m_sends:
        copy.wait_send()


def product_kernel(cols, scale, a_ref, b_ref, out_ref, x_ref, *accs):
    g = pl.program_id(0)
    group = lax.broadcasted_iota(I32, (8, 128), 1) // 32
    half = lax.broadcasted_iota(I32, (32, 128), 1) // 32

    @pl.when(g == 0)
    def _():
        def clear(t, _):
            for acc in accs:
                acc[pl.ds(t * 8, 8)] = jnp.zeros((8, 8, 128), F32)
            return _

        lax.fori_loop(0, 64, clear, 0)

    @pl.when(g < 16)
    def _():
        def products(i, _):
            a = a_ref[0, 0, i]
            zero = jnp.zeros_like(a)
            left = jnp.concatenate([jnp.where(half == m, a, zero) for m in range(4)], axis=0)
            right = b_ref[0, 0, pl.ds(i * 4, 4)].reshape(128, 128)
            prod = jnp.dot(left, right, preferred_element_type=F32)
            for m in range(4):
                rows = [prod[m * 32 + h * 8:m * 32 + h * 8 + 8, :] for h in range(4)]
                for n, block in enumerate(lane_groups(rows, group)):
                    x_ref[i, m * 4 + n] = block
            return _

        lax.fori_loop(0, 8, products, 0)

        def scatter(w, _):
            m, n = w // 4, w % 4
            for i, acc in enumerate(accs):
                row, lane = 2 * g + i // 4, ((i % 4) * 4 + m) * 8 + n
                j = cols[row, lane + 4]
                acc[j] = acc[j] + x_ref[i, w] * scale[row, lane]
            return _

        lax.fori_loop(0, 16, scatter, 0)

    for i, acc in enumerate(accs):
        @pl.when(g == 16 + i)
        def _(acc=acc):
            def tile(jt, _):
                w = lane_groups([acc[jt * 4 + n] for n in range(4)], group)
                lanes = pl.ds(pl.multiple_of(jt * 128, 128), 128)
                out_ref[0, :, lanes] = jnp.concatenate(w, axis=0).astype(BF16)
                return _

            lax.fori_loop(0, 128, tile, 0)


def on_device(a_blocks, a_scale, a_cols, b_blocks, b_scale, b_cols):
    vmem = pl.BlockSpec(memory_space=pltpu.VMEM)
    hbm = pl.BlockSpec(memory_space=pl.ANY)
    dma = pltpu.SemaphoreType.DMA
    brecv, arecv, cols, scale = pl.pallas_call(
        exchange_kernel,
        name="exchange",
        out_shape=(
            jax.ShapeDtypeStruct((8, 2, 32, 32, 128), BF16),
            jax.ShapeDtypeStruct((8, 2, 8, 32, 128), BF16),
            jax.ShapeDtypeStruct((32, 128), I32),
            jax.ShapeDtypeStruct((32, 128), F32),
        ),
        in_specs=[vmem, vmem, vmem, hbm, vmem, vmem],
        out_specs=(hbm, hbm, vmem, vmem),
        scratch_shapes=[
            pltpu.VMEM((512, 32, 128), BF16),
            pltpu.VMEM((8, 2, 32, 32, 128), BF16),
            pltpu.VMEM((8, 128), I32),
            pltpu.VMEM((8, 8, 128), I32),
            pltpu.VMEM((8, 128), F32),
            pltpu.VMEM((8, 8, 128), F32),
            pltpu.SMEM((8, 8, 128), I32),
            pltpu.SMEM((8, 8, 128), F32),
            pltpu.VMEM((512, 128), F32),
            pltpu.VMEM((8, 2, 8, 128), F32),
            pltpu.VMEM((8, 2, 8, 128), F32),
            dma((5,)), dma((7,)), dma((8,)), dma((7,)), dma((8,)),
            dma((15,)), dma((8, 2)), dma((15,)), dma((8, 2)), dma((9,)), dma((9,)),
        ],
        compiler_params=pltpu.CompilerParams(collective_id=0, has_side_effects=True, vmem_limit_bytes=32 << 20),
    )(a_cols[0, 0].T, a_scale[0, 0].T, a_blocks[0, 0], b_blocks[0, 0], b_scale[0, 0].T, b_cols[0, 0].T)
    out = pl.pallas_call(
        product_kernel,
        name="products",
        grid=(24,),
        out_shape=jax.ShapeDtypeStruct((8, 32, 16384), BF16),
        in_specs=[
            pl.BlockSpec(memory_space=pltpu.SMEM),
            pl.BlockSpec(memory_space=pltpu.SMEM),
            pl.BlockSpec((1, 1, 8, 32, 128), lambda g: (jnp.minimum(g, 15) // 2, jnp.minimum(g, 15) % 2, 0, 0, 0)),
            pl.BlockSpec((1, 1, 32, 32, 128), lambda g: (jnp.minimum(g, 15) // 2, jnp.minimum(g, 15) % 2, 0, 0, 0)),
        ],
        out_specs=pl.BlockSpec((1, 32, 16384), lambda g: (jnp.maximum(g - 16, 0), 0, 0)),
        scratch_shapes=[pltpu.VMEM((8, 16, 8, 128), F32)] + [pltpu.VMEM((512, 8, 128), F32)] * 8,
        compiler_params=pltpu.CompilerParams(vmem_limit_bytes=32 << 20),
    )(cols, scale, arecv, brecv)
    return out[None, None]


def solution(mesh):
    blocks = P("col", "row", None, None, None)
    small = P("col", "row", None, None)
    return jax.shard_map(
        on_device,
        mesh=mesh,
        in_specs=(blocks, small, small, blocks, small, small),
        out_specs=blocks,
        check_vma=False,
    )
```

```python
import jax
import jax.numpy as jnp
from jax import lax
from jax.experimental import pallas as pl
from jax.experimental.pallas import tpu as pltpu
from jax.sharding import PartitionSpec as P

MESH = pl.DeviceIdType.MESH
F32, BF16, I32 = jnp.float32, jnp.bfloat16, jnp.int32

OFFSETS = ((1, 0), (0, 1), (3, 0), (1, 1), (2, 0), (3, 1), (2, 1), (0, 0))
HOPS = (1, 3, 2)


def lane_groups(v, group):
    low, high = group % 2 == 0, group < 2
    t = [None] * 4
    for i in (0, 2):
        t[i] = jnp.where(low, v[i], pltpu.roll(v[i + 1], 32, 1))
        t[i + 1] = jnp.where(low, pltpu.roll(v[i], 96, 1), v[i + 1])
    w = [None] * 4
    for i in (0, 1):
        w[i] = jnp.where(high, t[i], pltpu.roll(t[i + 2], 64, 1))
        w[i + 2] = jnp.where(high, pltpu.roll(t[i], 64, 1), t[i + 2])
    return w


def exchange_kernel(
    cols_ref, scale_ref, a_ref, b_ref, bs_ref, bc_ref,
    xout, ocols,
    b_vm, a_vm, bs_vm, bc_vm, cols_vm, scale_vm, bsend, brecv, arecv, xs,
    idx_s, idx_r, as_s, as_r, idx_sm, as_sm, ctable, stable, msend, mrecv, m_sm,
    local_sem, out_sem, msm_sem, idx_ss, idx_rs, as_ss, as_rs, b_ss, b_rs, m_ss, m_rs, a_ss, a_rs,
):
    c, r = lax.axis_index("col"), lax.axis_index("row")
    s, q = c // 2, c % 2
    z, xl, y, xh = s // 2, s % 2, r // 2, r % 2
    k = (s + r) % 8
    rx = y * 2 + (1 - xh)
    kx = (s + rx) % 8

    def dev(s_, q_, r_):
        return {"row": r_, "col": 2 * s_ + q_}

    def chip(d):
        dz, dx = OFFSETS[d]
        return ((z + dz) % 4) * 2 + (1 - xl if dx else xl)

    def chip_behind(d):
        dz, dx = OFFSETS[d]
        return ((z + 4 - dz) % 4) * 2 + (1 - xl if dx else xl)

    def row_at(dy):
        return ((y + dy) % 4) * 2 + xh

    def send(src, dst, ssem, rsem, target):
        return pltpu.make_async_remote_copy(
            src_ref=src, dst_ref=dst, send_sem=ssem, recv_sem=rsem, device_id=target, device_id_type=MESH
        )

    loads = [
        pltpu.make_async_copy(src, dst, local_sem.at[n])
        for n, (src, dst) in enumerate(
            ((cols_ref, cols_vm), (scale_ref, scale_vm), (a_ref, a_vm), (bs_ref, bs_vm), (bc_ref, bc_vm), (b_ref, b_vm))
        )
    ]
    for copy in loads:
        copy.start()

    barrier = pltpu.get_barrier_semaphore()
    peers = []
    for e in range(1, 8):
        peers.append(dev((s + 8 - e) % 8, q, (r + e) % 8))
    for d in range(7):
        for p in range(2):
            peers.append(dev(chip(d), p, r))
    peers.append(dev(s, 1 - q, r))
    for p in range(2):
        peers.append(dev(s, p, rx))
    for dy in HOPS:
        peers.append(dev(s, q, row_at(dy)))
    for peer in peers:
        pl.semaphore_signal(barrier, inc=1, device_id=peer, device_id_type=MESH)
    idx_s[...] = jnp.zeros_like(idx_s)
    as_s[...] = jnp.zeros_like(as_s)
    loads[0].wait()
    loads[1].wait()
    idx_s[0:4, 0:16] = cols_vm[...]
    as_s[0:4, 0:16] = scale_vm[...]
    loads[2].wait()
    pl.semaphore_wait(barrier, len(peers))

    idx_sends = []
    for e in range(1, 8):
        to = dev((s + 8 - e) % 8, q, (r + e) % 8)
        idx_sends.append(send(idx_s, idx_r.at[s], idx_ss.at[e - 1], idx_rs.at[s], to))
        idx_sends.append(send(as_s, as_r.at[s], as_ss.at[e - 1], as_rs.at[s], to))
    for copy in idx_sends:
        copy.start()

    own_rows = pl.ds(pl.multiple_of(q * 8, 8), 8)
    other_half = a_vm.at[pl.ds(pl.multiple_of((1 - q) * 8, 8), 8)]
    a_sends = [send(a_vm.at[pl.ds(p * 8, 8)], arecv.at[k, q], a_ss.at[1 + p], a_rs.at[1 + q], dev(s, p, rx)) for p in range(2)]
    a_sends.append(send(other_half, arecv.at[k, q], a_ss.at[0], a_rs.at[0], dev(s, 1 - q, r)))
    for copy in a_sends:
        copy.start()
    arecv[k, q] = a_vm[own_rows]

    idx_r[s] = idx_s[...]
    as_r[s] = as_s[...]
    loads[3].wait()
    loads[4].wait()
    for g in range(4):
        lanes = pl.ds(g * 128, 128)
        for src, table in ((bs_vm, stable), (bc_vm, ctable)):
            v = src[:, lanes].astype(F32)
            eights = [jnp.broadcast_to(v[n:n + 1, :], (8, 128)) for n in range(4)]
            table[lanes, :] = jnp.transpose(jnp.concatenate(eights * 4, axis=0))

    for e in range(1, 8):
        sb, rb = (s + e) % 8, (r + 8 - e) % 8
        send(idx_s, idx_r.at[sb], idx_ss.at[e - 1], idx_rs.at[sb], dev(sb, q, rb)).wait_recv()
        send(as_s, as_r.at[sb], as_ss.at[e - 1], as_rs.at[sb], dev(sb, q, rb)).wait_recv()
    to_smem = [pltpu.make_async_copy(idx_r, idx_sm, local_sem.at[6]), pltpu.make_async_copy(as_r, as_sm, local_sem.at[7])]
    for copy in to_smem:
        copy.start()
    for copy in to_smem:
        copy.wait()
    loads[5].wait()

    lane = lax.broadcasted_iota(I32, (1, 128), 1)
    slot_m, slot_i = lane // 32, lane % 8

    def metas(sd, p, out):
        def row_of(i, rows):
            srow, crow = rows
            for m in range(4):
                t = idx_sm[sd, m, p * 8 + i]
                here = (slot_m == m) & (slot_i == i)
                srow = jnp.where(here, stable[pl.ds(t, 1), :] * as_sm[sd, m, p * 8 + i], srow)
                crow = jnp.where(here, ctable[pl.ds(t, 1), :], crow)
            return srow, crow

        empty = jnp.zeros((1, 128), F32)
        srow, crow = lax.fori_loop(0, 8, row_of, (empty, empty))
        out[0:1, :] = srow
        out[1:2, :] = crow * 8.0

    def gather(sd, p, out):
        def rows_of(i, _):
            for m in range(4):
                out[i * 4 + m] = b_vm[idx_sm[sd, m, p * 8 + i]]
            return _

        lax.fori_loop(0, 8, rows_of, 0)

    b_sends, m_sends = [], []
    pending = []
    for d in range(7):
        sd = chip(d)
        for p in range(2):
            n = 2 * d + p
            gather(sd, p, bsend.at[n])
            metas(sd, p, msend.at[n])
            for copy in pending:
                copy.start()
            m_copy = send(msend.at[n], mrecv.at[k, q], m_ss.at[n], m_rs.at[k, q], dev(sd, p, r))
            b_copy = send(bsend.at[n], brecv.at[k, q], b_ss.at[n], b_rs.at[k, q], dev(sd, p, r))
            m_sends.append(m_copy)
            b_sends.append(b_copy)
            pending = [m_copy, b_copy]
    gather(s, 1 - q, bsend.at[14])
    metas(s, 1 - q, msend.at[14])
    for copy in pending:
        copy.start()
    gather(s, q, brecv.at[k, q])
    metas(s, q, mrecv.at[k, q])
    m_copy = send(msend.at[14], mrecv.at[k, q], m_ss.at[14], m_rs.at[k, q], dev(s, 1 - q, r))
    b_copy = send(bsend.at[14], brecv.at[k, q], b_ss.at[14], b_rs.at[k, q], dev(s, 1 - q, r))
    m_sends.append(m_copy)
    b_sends.append(b_copy)
    m_copy.start()
    b_copy.start()

    send(other_half, arecv.at[k, 1 - q], a_ss.at[0], a_rs.at[0], dev(s, 1 - q, r)).wait_recv()
    for p in range(2):
        send(other_half, arecv.at[kx, p], a_ss.at[1 + p], a_rs.at[1 + p], dev(s, p, rx)).wait_recv()
    for h, dy in enumerate(HOPS):
        for j, slot in enumerate((k, kx)):
            n = 3 + 2 * h + j
            copy = send(arecv.at[slot], arecv.at[slot], a_ss.at[n], a_rs.at[n], dev(s, q, row_at(dy)))
            copy.start()
            a_sends.append(copy)

    group = lax.broadcasted_iota(I32, (8, 128), 1) // 32
    quarter = lax.broadcasted_iota(I32, (32, 128), 1) // 32
    outs = []

    def process(kb, p):
        e = len(outs)
        scales = pltpu.make_async_copy(mrecv.at[kb, p], m_sm.at[e], msm_sem.at[e])
        scales.start()
        ocols[e:e + 1, :] = mrecv[kb, p, 1:2, :].astype(I32)
        return e, scales

    def products(e, scales, kb, p):
        scales.wait()
        if e >= 2:
            outs[e - 2].wait()
        x = xs.at[e % 2]

        def row(i, _):
            a = arecv[kb, p, i]
            zero = jnp.zeros_like(a)
            left = jnp.concatenate([jnp.where(quarter == m, a, zero) for m in range(4)], axis=0)
            right = brecv[kb, p, pl.ds(i * 4, 4)].reshape(128, 128)
            prod = jnp.dot(left, right, preferred_element_type=F32)
            for m in range(4):
                rows = [prod[m * 32 + h * 8:m * 32 + h * 8 + 8, :] for h in range(4)]
                for n, block in enumerate(lane_groups(rows, group)):
                    w = m * 4 + n
                    x[i, w] = block * m_sm[e, 0, w * 8 + i]
            return _

        lax.fori_loop(0, 8, row, 0)
        copy = pltpu.make_async_copy(x, xout.at[e], out_sem.at[e])
        copy.start()
        outs.append(copy)

    e, scales = process(k, q)
    products(e, scales, k, q)
    n_other = 1 - q
    send(msend.at[14], mrecv.at[k, n_other], m_ss.at[14], m_rs.at[k, n_other], dev(s, n_other, r)).wait_recv()
    e, scales = process(k, n_other)
    send(bsend.at[14], brecv.at[k, n_other], b_ss.at[14], b_rs.at[k, n_other], dev(s, n_other, r)).wait_recv()
    products(e, scales, k, n_other)
    for h, dy in enumerate(HOPS):
        rb = row_at(4 - dy)
        for j, rr in enumerate((rb, (rb // 2) * 2 + (1 - xh))):
            slot = (s + rr) % 8
            n = 3 + 2 * h + j
            send(arecv.at[slot], arecv.at[slot], a_ss.at[n], a_rs.at[n], dev(s, q, rb)).wait_recv()
    for d in range(7):
        sb = chip_behind(d)
        kb = (sb + r) % 8
        for p in range(2):
            n = 2 * d + p
            send(msend.at[n], mrecv.at[kb, p], m_ss.at[n], m_rs.at[kb, p], dev(sb, p, r)).wait_recv()
            e, scales = process(kb, p)
            send(bsend.at[n], brecv.at[kb, p], b_ss.at[n], b_rs.at[kb, p], dev(sb, p, r)).wait_recv()
            products(e, scales, kb, p)
    for copy in idx_sends + a_sends + b_sends + m_sends:
        copy.wait_send()
    for copy in outs[14:]:
        copy.wait()


def scatter_kernel(cols, x_ref, out_ref, *accs):
    g = pl.program_id(0)
    group = lax.broadcasted_iota(I32, (8, 128), 1) // 32

    @pl.when(g == 0)
    def _():
        def clear(t, _):
            for acc in accs:
                acc[pl.ds(t * 64, 64), :] = jnp.zeros((64, 128), F32)
            return _

        lax.fori_loop(0, 64, clear, 0)

    @pl.when(g < 16)
    def _():
        def scatter(w4, _):
            for ww in range(4):
                w = w4 * 4 + ww
                at = [pl.ds(pl.multiple_of(cols[g, w * 8 + i], 8), 8) for i in range(8)]
                new = [acc[at[i], :] + x_ref[0, i, w] for i, acc in enumerate(accs)]
                for i, acc in enumerate(accs):
                    acc[at[i], :] = new[i]
            return _

        lax.fori_loop(0, 4, scatter, 0)

    for i, acc in enumerate(accs):
        @pl.when(g == 16 + i)
        def _(acc=acc):
            def tile(t, _):
                tiles = []
                for u in range(8):
                    base = pl.multiple_of((t * 8 + u) * 32, 32)
                    tiles.append(lane_groups([acc[pl.ds(base + n * 8, 8), :] for n in range(4)], group))
                for h in range(4):
                    row = jnp.concatenate([w[h] for w in tiles], axis=1).astype(BF16)
                    out_ref[0, h * 8:h * 8 + 8, pl.ds(pl.multiple_of(t * 1024, 1024), 1024)] = row
                return _

            lax.fori_loop(0, 16, tile, 0)


def on_device(a_blocks, a_scale, a_cols, b_blocks, b_scale, b_cols):
    hbm = pl.BlockSpec(memory_space=pltpu.HBM)
    dma = pltpu.SemaphoreType.DMA
    x, cols = pl.pallas_call(
        exchange_kernel,
        name="exchange",
        out_shape=(
            jax.ShapeDtypeStruct((16, 8, 16, 8, 128), F32),
            jax.ShapeDtypeStruct((16, 128), I32),
        ),
        in_specs=[hbm] * 6,
        out_specs=(hbm, pl.BlockSpec(memory_space=pltpu.VMEM)),
        scratch_shapes=[
            pltpu.VMEM((512, 32, 128), BF16),
            pltpu.VMEM((16, 32, 128), BF16),
            pltpu.VMEM((4, 512), F32),
            pltpu.VMEM((4, 512), I32),
            pltpu.VMEM((4, 16), I32),
            pltpu.VMEM((4, 16), F32),
            pltpu.VMEM((15, 32, 32, 128), BF16),
            pltpu.VMEM((8, 2, 32, 32, 128), BF16),
            pltpu.VMEM((8, 2, 8, 32, 128), BF16),
            pltpu.VMEM((2, 8, 16, 8, 128), F32),
            pltpu.VMEM((8, 128), I32),
            pltpu.VMEM((8, 8, 128), I32),
            pltpu.VMEM((8, 128), F32),
            pltpu.VMEM((8, 8, 128), F32),
            pltpu.SMEM((8, 8, 128), I32),
            pltpu.SMEM((8, 8, 128), F32),
            pltpu.VMEM((512, 128), F32),
            pltpu.VMEM((512, 128), F32),
            pltpu.VMEM((15, 8, 128), F32),
            pltpu.VMEM((8, 2, 8, 128), F32),
            pltpu.SMEM((16, 8, 128), F32),
            dma((8,)), dma((16,)), dma((16,)), dma((7,)), dma((8,)), dma((7,)), dma((8,)),
            dma((15,)), dma((8, 2)), dma((15,)), dma((8, 2)), dma((9,)), dma((9,)),
        ],
        compiler_params=pltpu.CompilerParams(collective_id=0, has_side_effects=True, vmem_limit_bytes=67043328),
    )(a_cols[0, 0].T, a_scale[0, 0].T, a_blocks[0, 0], b_blocks[0, 0], b_scale[0, 0].T, b_cols[0, 0].T)
    out = pl.pallas_call(
        scatter_kernel,
        name="scatter",
        grid=(24,),
        out_shape=jax.ShapeDtypeStruct((8, 32, 16384), BF16),
        in_specs=[
            pl.BlockSpec(memory_space=pltpu.SMEM),
            pl.BlockSpec((1, 8, 16, 8, 128), lambda g: (jnp.minimum(g, 15), 0, 0, 0, 0)),
        ],
        out_specs=pl.BlockSpec((1, 32, 16384), lambda g: (jnp.maximum(g - 16, 0), 0, 0)),
        scratch_shapes=[pltpu.VMEM((4096, 128), F32)] * 8,
        compiler_params=pltpu.CompilerParams(vmem_limit_bytes=32 << 20),
    )(cols, x)
    return out[None, None]


def solution(mesh):
    blocks = P("col", "row", None, None, None)
    small = P("col", "row", None, None)
    return jax.shard_map(
        on_device,
        mesh=mesh,
        in_specs=(blocks, small, small, blocks, small, small),
        out_specs=blocks,
        check_vma=False,
    )
```

```python
import jax
import jax.numpy as jnp
from jax import lax
from jax.experimental import pallas as pl
from jax.experimental.pallas import tpu as pltpu
from jax.sharding import PartitionSpec as P

MESH = pl.DeviceIdType.MESH
F32, BF16, I32 = jnp.float32, jnp.bfloat16, jnp.int32

HOPS = (1, 3, 2)
CHIPS = (0, 7, 3, 5, 6, 2, 4, 1)


def lane_groups(v, low, high):
    t = [None] * 4
    for i in (0, 2):
        t[i] = jnp.where(low, v[i], pltpu.roll(v[i + 1], 32, 1))
        t[i + 1] = jnp.where(low, pltpu.roll(v[i], 96, 1), v[i + 1])
    w = [None] * 4
    for i in (0, 1):
        w[i] = jnp.where(high, t[i], pltpu.roll(t[i + 2], 64, 1))
        w[i + 2] = jnp.where(high, pltpu.roll(t[i], 64, 1), t[i + 2])
    return w


def exchange_kernel(
    cols_ref, scale_ref, a_ref, b_ref, bs_ref, bc_ref,
    xout, ocols,
    b_vm, a_vm, bs_vm, bc_vm, cols_vm, scale_vm, bsend, brecv, arecv, prods, xs,
    idx_s, idx_r, as_s, as_r, idx_sm, as_sm, ctable, stable, msend, mrecv, m_sm,
    local_sem, out_sem, msm_sem, idx_ss, idx_rs, as_ss, as_rs, b_ss, b_rs, m_ss, m_rs, a_ss, a_rs,
):
    c, r = lax.axis_index("col"), lax.axis_index("row")
    s, q = c // 2, c % 2
    z, xl, y, xh = s // 2, s % 2, r // 2, r % 2
    k = (s + r) % 8
    rx = y * 2 + (1 - xh)
    kx = (s + rx) % 8

    def dev(s_, q_, r_):
        return {"row": r_, "col": 2 * s_ + q_}

    def hop(e):
        t = (e // 2) % 8
        f = t * 0
        for n, number in enumerate(CHIPS):
            f = jnp.where(t == n, number, f)
        dx, h = f % 2, f // 2
        return h + h // 2 - 2 * (h // 3), xl + dx - 2 * xl * dx

    def chip(e):
        dz, x = hop(e)
        return ((z + dz) % 4) * 2 + x

    def chip_behind(e):
        dz, x = hop(e)
        return ((z + 4 - dz) % 4) * 2 + x

    def core(e):
        return (q + e) % 2

    def row_at(dy):
        return ((y + dy) % 4) * 2 + xh

    def send(src, dst, ssem, rsem, target):
        return pltpu.make_async_remote_copy(
            src_ref=src, dst_ref=dst, send_sem=ssem, recv_sem=rsem, device_id=target, device_id_type=MESH
        )

    loads = [
        pltpu.make_async_copy(src, dst, local_sem.at[n])
        for n, (src, dst) in enumerate(
            ((cols_ref, cols_vm), (scale_ref, scale_vm), (a_ref, a_vm), (bs_ref, bs_vm), (bc_ref, bc_vm), (b_ref, b_vm))
        )
    ]
    for copy in loads:
        copy.start()

    barrier = pltpu.get_barrier_semaphore()
    peers = []
    for e in range(1, 8):
        peers.append(dev((s + 8 - e) % 8, q, (r + e) % 8))
    for e in range(1, 16):
        peers.append(dev(chip(e), core(e), r))
    for p in range(2):
        peers.append(dev(s, p, rx))
    for dy in HOPS:
        peers.append(dev(s, q, row_at(dy)))
    for peer in peers:
        pl.semaphore_signal(barrier, inc=1, device_id=peer, device_id_type=MESH)
    idx_s[...] = jnp.zeros_like(idx_s)
    as_s[...] = jnp.zeros_like(as_s)
    loads[0].wait()
    loads[1].wait()
    for p in range(2):
        idx_s[p * 4:p * 4 + 4, 0:8] = cols_vm[:, p * 8:p * 8 + 8]
        as_s[p * 4:p * 4 + 4, 0:8] = scale_vm[:, p * 8:p * 8 + 8]
    loads[2].wait()
    pl.semaphore_wait(barrier, len(peers))

    idx_sends = []
    for e in range(1, 8):
        to = dev((s + 8 - e) % 8, q, (r + e) % 8)
        idx_sends.append(send(idx_s, idx_r.at[s], idx_ss.at[e - 1], idx_rs.at[s], to))
        idx_sends.append(send(as_s, as_r.at[s], as_ss.at[e - 1], as_rs.at[s], to))
    for copy in idx_sends:
        copy.start()

    own_rows = pl.ds(pl.multiple_of(q * 8, 8), 8)
    other_half = a_vm.at[pl.ds(pl.multiple_of((1 - q) * 8, 8), 8)]
    a_sends = [send(a_vm.at[pl.ds(p * 8, 8)], arecv.at[k, q], a_ss.at[1 + p], a_rs.at[1 + q], dev(s, p, rx)) for p in range(2)]
    a_sends.append(send(other_half, arecv.at[k, q], a_ss.at[0], a_rs.at[0], dev(s, 1 - q, r)))
    for copy in a_sends:
        copy.start()
    arecv[k, q] = a_vm[own_rows]

    idx_r[s] = idx_s[...]
    as_r[s] = as_s[...]
    loads[3].wait()
    loads[4].wait()
    for g in range(4):
        lanes = pl.ds(g * 128, 128)
        for src, table in ((bs_vm, stable), (bc_vm, ctable)):
            v = src[:, lanes].astype(F32)
            eights = [jnp.broadcast_to(v[n:n + 1, :], (8, 128)) for n in range(4)]
            table[lanes, :] = jnp.transpose(jnp.concatenate(eights * 4, axis=0))

    for e in range(1, 8):
        sb, rb = (s + e) % 8, (r + 8 - e) % 8
        send(idx_s, idx_r.at[sb], idx_ss.at[e - 1], idx_rs.at[sb], dev(sb, q, rb)).wait_recv()
        send(as_s, as_r.at[sb], as_ss.at[e - 1], as_rs.at[sb], dev(sb, q, rb)).wait_recv()
    to_smem = [pltpu.make_async_copy(idx_r, idx_sm, local_sem.at[6]), pltpu.make_async_copy(as_r, as_sm, local_sem.at[7])]
    for copy in to_smem:
        copy.start()
    for copy in to_smem:
        copy.wait()
    loads[5].wait()

    lane = lax.broadcasted_iota(I32, (1, 128), 1)
    place = lane // 32 * 8 + lane % 8

    def to_peer(e):
        target = dev(chip(e), core(e), r)
        n = e - 2
        return (
            send(msend.at[n], mrecv.at[k, q], m_ss.at[n], m_rs.at[k, q], target),
            send(bsend.at[n], brecv.at[k, q], b_ss.at[n], b_rs.at[k, q], target),
        )

    def pick(e, carry):
        sd, p, n = chip(e), core(e), e - 2
        srow = crow = jnp.zeros((1, 128), F32)
        for i in range(8):
            for m in range(4):
                t = idx_sm[sd, p * 4 + m, i]
                bsend[n, i * 4 + m] = b_vm[t]
                here = place == m * 8 + i
                srow = jnp.where(here, stable[pl.ds(t, 1), :] * as_sm[sd, p * 4 + m, i], srow)
                crow = jnp.where(here, ctable[pl.ds(t, 1), :], crow)
        msend[n, 0:1, :] = srow
        msend[n, 1:2, :] = crow * 8.0

        @pl.when((e > 2) & (e < 17))
        def _():
            for copy in to_peer(e - 1):
                copy.start()

        return carry

    lax.fori_loop(2, 18, pick, 0)
    for copy in to_peer(17):
        copy.start()
    own = [
        pltpu.make_async_copy(msend.at[14], mrecv.at[k, q], local_sem.at[8]),
        pltpu.make_async_copy(bsend.at[14], brecv.at[k, q], local_sem.at[9]),
    ]
    for copy in own:
        copy.start()

    send(other_half, arecv.at[k, 1 - q], a_ss.at[0], a_rs.at[0], dev(s, 1 - q, r)).wait_recv()
    for p in range(2):
        send(other_half, arecv.at[kx, p], a_ss.at[1 + p], a_rs.at[1 + p], dev(s, p, rx)).wait_recv()
    for h, dy in enumerate(HOPS):
        for j, slot in enumerate((k, kx)):
            n = 3 + 2 * h + j
            copy = send(arecv.at[slot], arecv.at[slot], a_ss.at[n], a_rs.at[n], dev(s, q, row_at(dy)))
            copy.start()
            a_sends.append(copy)
    for copy in own:
        copy.wait()

    group = lax.broadcasted_iota(I32, (8, 128), 1) // 32
    low, high = group % 2 == 0, group < 2
    quarter = lax.broadcasted_iota(I32, (32, 128), 1) // 32

    def out_copy(e):
        return pltpu.make_async_copy(xs.at[e % 2], xout.at[e], out_sem.at[e])

    def process(e, carry):
        sb, p = chip_behind(e), core(e)
        kb = (sb + r) % 8
        source = dev(sb, p, r)

        @pl.when(e > 0)
        def _():
            send(msend.at[0], mrecv.at[kb, p], m_ss.at[0], m_rs.at[kb, p], source).wait_recv()

        scales = pltpu.make_async_copy(mrecv.at[kb, p], m_sm.at[e], msm_sem.at[e])
        scales.start()
        ocols[pl.ds(e, 1), :] = mrecv[kb, p, 1:2, :].astype(I32)

        @pl.when(e == 2)
        def _():
            for h, dy in enumerate(HOPS):
                rb = row_at(4 - dy)
                for j, rr in enumerate((rb, (rb // 2) * 2 + (1 - xh))):
                    slot = (s + rr) % 8
                    n = 3 + 2 * h + j
                    send(arecv.at[slot], arecv.at[slot], a_ss.at[n], a_rs.at[n], dev(s, q, rb)).wait_recv()

        @pl.when(e > 0)
        def _():
            send(bsend.at[0], brecv.at[kb, p], b_ss.at[0], b_rs.at[kb, p], source).wait_recv()

        for i in range(8):
            a = arecv[kb, p, i]
            zero = jnp.zeros_like(a)
            left = jnp.concatenate([jnp.where(quarter == m, a, zero) for m in range(4)], axis=0)
            right = brecv[kb, p, i * 4:i * 4 + 4].reshape(128, 128)
            prods[i] = jnp.dot(left, right, preferred_element_type=F32)
        scales.wait()

        @pl.when(e >= 2)
        def _():
            out_copy(e - 2).wait()

        for i in range(8):
            for m in range(4):
                rows = [prods[i, m * 32 + h * 8:m * 32 + h * 8 + 8, :] for h in range(4)]
                for n, block in enumerate(lane_groups(rows, low, high)):
                    w = m * 4 + n
                    xs[e % 2, i, w] = block * m_sm[e, 0, w * 8 + i]
        out_copy(e).start()
        return carry

    lax.fori_loop(0, 16, process, 0)
    for copy in idx_sends + a_sends:
        copy.wait_send()
    for e in range(2, 18):
        if e != 16:
            for copy in to_peer(e):
                copy.wait_send()
    for e in (14, 15):
        out_copy(e).wait()


def scatter_kernel(cols, x_ref, out_ref, x, sem, *accs):
    g = pl.program_id(0)

    @pl.when(g == 0)
    def _():
        def load(e):
            return pltpu.make_async_copy(x_ref.at[e], x.at[e], sem.at[e])

        for e in range(16):
            load(e).start()

        def clear(t, _):
            for acc in accs:
                acc[pl.ds(pl.multiple_of(t * 64, 64), 64), :] = jnp.zeros((64, 128), F32)
            return _

        lax.fori_loop(0, 64, clear, 0)

        def add(e, _):
            load(e).wait()
            for w in range(16):
                at = [pl.ds(pl.multiple_of(cols[e, w * 8 + i], 8), 8) for i in range(8)]
                new = [acc[at[i], :] + x[e, i, w] for i, acc in enumerate(accs)]
                for i, acc in enumerate(accs):
                    acc[at[i], :] = new[i]
            return _

        lax.fori_loop(0, 16, add, 0)

    group = lax.broadcasted_iota(I32, (16, 128), 1) // 32
    low, high = group % 2 == 0, group < 2
    for i, acc in enumerate(accs):
        @pl.when(g == i)
        def _(acc=acc):
            def tile(t, _):
                for u in range(8):
                    base = pl.multiple_of((t * 8 + u) * 64, 64)
                    v = [
                        jnp.concatenate([acc[pl.ds(base + n * 8, 8), :], acc[pl.ds(base + 32 + n * 8, 8), :]], axis=0).astype(BF16)
                        for n in range(4)
                    ]
                    w = lane_groups(v, low, high)
                    for h in range(4):
                        lanes = pl.ds(pl.multiple_of((t * 8 + u) * 256, 256), 256)
                        out_ref[0, h * 8:h * 8 + 8, lanes] = jnp.concatenate([w[h][0:8], w[h][8:16]], axis=1)
                return _

            lax.fori_loop(0, 8, tile, 0)


def on_device(a_blocks, a_scale, a_cols, b_blocks, b_scale, b_cols):
    hbm = pl.BlockSpec(memory_space=pltpu.HBM)
    dma = pltpu.SemaphoreType.DMA
    x, cols = pl.pallas_call(
        exchange_kernel,
        name="exchange",
        out_shape=(
            jax.ShapeDtypeStruct((16, 8, 16, 8, 128), F32),
            jax.ShapeDtypeStruct((16, 128), I32),
        ),
        in_specs=[hbm] * 6,
        out_specs=(hbm, pl.BlockSpec(memory_space=pltpu.VMEM)),
        scratch_shapes=[
            pltpu.VMEM((512, 32, 128), BF16),
            pltpu.VMEM((16, 32, 128), BF16),
            pltpu.VMEM((4, 512), F32),
            pltpu.VMEM((4, 512), I32),
            pltpu.VMEM((4, 16), I32),
            pltpu.VMEM((4, 16), F32),
            pltpu.VMEM((16, 32, 32, 128), BF16),
            pltpu.VMEM((8, 2, 32, 32, 128), BF16),
            pltpu.VMEM((8, 2, 8, 32, 128), BF16),
            pltpu.VMEM((8, 128, 128), F32),
            pltpu.VMEM((2, 8, 16, 8, 128), F32),
            pltpu.VMEM((8, 128), I32),
            pltpu.VMEM((8, 8, 128), I32),
            pltpu.VMEM((8, 128), F32),
            pltpu.VMEM((8, 8, 128), F32),
            pltpu.SMEM((8, 8, 128), I32),
            pltpu.SMEM((8, 8, 128), F32),
            pltpu.VMEM((512, 128), F32),
            pltpu.VMEM((512, 128), F32),
            pltpu.VMEM((16, 8, 128), F32),
            pltpu.VMEM((8, 2, 8, 128), F32),
            pltpu.SMEM((16, 8, 128), F32),
            dma((10,)), dma((16,)), dma((16,)), dma((7,)), dma((8,)), dma((7,)), dma((8,)),
            dma((16,)), dma((8, 2)), dma((16,)), dma((8, 2)), dma((9,)), dma((9,)),
        ],
        compiler_params=pltpu.CompilerParams(collective_id=0, has_side_effects=True, vmem_limit_bytes=67043328),
    )(a_cols[0, 0].T, a_scale[0, 0].T, a_blocks[0, 0], b_blocks[0, 0], b_scale[0, 0].T, b_cols[0, 0].T)
    out = pl.pallas_call(
        scatter_kernel,
        name="scatter",
        grid=(8,),
        out_shape=jax.ShapeDtypeStruct((8, 32, 16384), BF16),
        in_specs=[pl.BlockSpec(memory_space=pltpu.SMEM), hbm],
        out_specs=pl.BlockSpec((1, 32, 16384), lambda g: (g, 0, 0)),
        scratch_shapes=[pltpu.VMEM((16, 8, 16, 8, 128), F32), dma((16,))] + [pltpu.VMEM((4096, 128), F32)] * 8,
        compiler_params=pltpu.CompilerParams(vmem_limit_bytes=67043328),
    )(cols, x)
    return out[None, None]


def solution(mesh):
    blocks = P("col", "row", None, None, None)
    small = P("col", "row", None, None)
    return jax.shard_map(
        on_device,
        mesh=mesh,
        in_specs=(blocks, small, small, blocks, small, small),
        out_specs=blocks,
        check_vma=False,
    )
```

```python
import jax
import jax.numpy as jnp
from jax import lax
from jax.experimental import pallas as pl
from jax.experimental.pallas import tpu as pltpu
from jax.sharding import PartitionSpec as P

MESH = pl.DeviceIdType.MESH
F32, BF16, I32 = jnp.float32, jnp.bfloat16, jnp.int32

HOPS = (1, 3, 2)
CHIPS = (0, 7, 6, 3, 5, 2, 4, 1)


def lane_groups(v, low, high):
    t, w = [None] * 4, [None] * 4
    for i in (0, 2):
        turned = pltpu.roll(jnp.where(low, v[i + 1], v[i]), 32, 1)
        t[i], t[i + 1] = jnp.where(low, v[i], turned), jnp.where(low, turned, v[i + 1])
    for i in (0, 1):
        turned = pltpu.roll(jnp.where(high, t[i + 2], t[i]), 64, 1)
        w[i], w[i + 2] = jnp.where(high, t[i], turned), jnp.where(high, turned, t[i + 2])
    return [w[0], jnp.where(low, w[3], w[1]), w[2], jnp.where(low, w[1], w[3])]


def exchange_kernel(
    cols_ref, scale_ref, a_ref, b_ref, bs_ref, bc_ref,
    xout, ocols,
    b_vm, a_vm, bs_vm, bc_vm, cols_vm, scale_vm, bsend, brecv, arecv, prods, xs,
    idx_s, idx_r, as_s, as_r, idx_sm, as_sm, ctable, stable, msend, mrecv, m_sm,
    local_sem, out_sem, msm_sem, idx_ss, idx_rs, as_ss, as_rs, b_ss, b_rs, m_ss, m_rs, a_ss, a_rs,
):
    c, r = lax.axis_index("col"), lax.axis_index("row")
    s, q = c // 2, c % 2
    z, xl, y, xh = s // 2, s % 2, r // 2, r % 2
    k = (s + r) % 8
    rx = y * 2 + (1 - xh)
    kx = (s + rx) % 8

    def dev(s_, q_, r_):
        return {"row": r_, "col": 2 * s_ + q_}

    def hop(e):
        t = (e // 2) % 8
        f = t * 0
        for n, number in enumerate(CHIPS):
            f = jnp.where(t == n, number, f)
        dx, h = f % 2, f // 2
        return h + h // 2 - 2 * (h // 3), xl + dx - 2 * xl * dx

    def chip(e):
        dz, x = hop(e)
        return ((z + dz) % 4) * 2 + x

    def chip_behind(e):
        dz, x = hop(e)
        return ((z + 4 - dz) % 4) * 2 + x

    def core(e):
        return (q + e) % 2

    def row_at(dy):
        return ((y + dy) % 4) * 2 + xh

    def send(src, dst, ssem, rsem, target):
        return pltpu.make_async_remote_copy(
            src_ref=src, dst_ref=dst, send_sem=ssem, recv_sem=rsem, device_id=target, device_id_type=MESH
        )

    loads = [
        pltpu.make_async_copy(src, dst, local_sem.at[n])
        for n, (src, dst) in enumerate(
            ((cols_ref, cols_vm), (scale_ref, scale_vm), (a_ref, a_vm), (bs_ref, bs_vm), (bc_ref, bc_vm), (b_ref, b_vm))
        )
    ]
    for copy in loads:
        copy.start()

    barrier = pltpu.get_barrier_semaphore()
    peers = []
    for e in range(1, 8):
        peers.append(dev((s + 8 - e) % 8, q, (r + e) % 8))
    for e in range(1, 16):
        peers.append(dev(chip(e), core(e), r))
    for p in range(2):
        peers.append(dev(s, p, rx))
    for dy in HOPS:
        peers.append(dev(s, q, row_at(dy)))
    for peer in peers:
        pl.semaphore_signal(barrier, inc=1, device_id=peer, device_id_type=MESH)
    idx_s[...] = jnp.zeros_like(idx_s)
    as_s[...] = jnp.zeros_like(as_s)
    loads[0].wait()
    loads[1].wait()
    for p in range(2):
        idx_s[p * 4:p * 4 + 4, 0:8] = cols_vm[:, p * 8:p * 8 + 8]
        as_s[p * 4:p * 4 + 4, 0:8] = scale_vm[:, p * 8:p * 8 + 8]
    loads[2].wait()
    pl.semaphore_wait(barrier, len(peers))

    idx_sends = []
    for e in range(1, 8):
        to = dev((s + 8 - e) % 8, q, (r + e) % 8)
        idx_sends.append(send(idx_s, idx_r.at[s], idx_ss.at[e - 1], idx_rs.at[s], to))
        idx_sends.append(send(as_s, as_r.at[s], as_ss.at[e - 1], as_rs.at[s], to))
    for copy in idx_sends:
        copy.start()

    own_rows = pl.ds(pl.multiple_of(q * 8, 8), 8)
    other_half = a_vm.at[pl.ds(pl.multiple_of((1 - q) * 8, 8), 8)]
    a_sends = [send(a_vm.at[pl.ds(p * 8, 8)], arecv.at[k, q], a_ss.at[1 + p], a_rs.at[1 + q], dev(s, p, rx)) for p in range(2)]
    a_sends.append(send(other_half, arecv.at[k, q], a_ss.at[0], a_rs.at[0], dev(s, 1 - q, r)))
    for copy in a_sends:
        copy.start()
    arecv[k, q] = a_vm[own_rows]

    idx_r[s] = idx_s[...]
    as_r[s] = as_s[...]
    loads[3].wait()
    loads[4].wait()
    for g in range(4):
        lanes = pl.ds(g * 128, 128)
        for src, table in ((bs_vm, stable), (bc_vm, ctable)):
            v = src[:, lanes].astype(F32)
            eights = [jnp.broadcast_to(v[n:n + 1, :], (8, 128)) for n in range(4)]
            table[lanes, :] = jnp.transpose(jnp.concatenate(eights * 4, axis=0))

    for e in range(1, 8):
        sb, rb = (s + e) % 8, (r + 8 - e) % 8
        send(idx_s, idx_r.at[sb], idx_ss.at[e - 1], idx_rs.at[sb], dev(sb, q, rb)).wait_recv()
        send(as_s, as_r.at[sb], as_ss.at[e - 1], as_rs.at[sb], dev(sb, q, rb)).wait_recv()
    to_smem = [pltpu.make_async_copy(idx_r, idx_sm, local_sem.at[6]), pltpu.make_async_copy(as_r, as_sm, local_sem.at[7])]
    for copy in to_smem:
        copy.start()
    for copy in to_smem:
        copy.wait()
    loads[5].wait()

    lane = lax.broadcasted_iota(I32, (1, 128), 1)
    place = lane // 32 * 8 + lane % 8

    def to_peer(e):
        target = dev(chip(e), core(e), r)
        n = e - 2
        return (
            send(msend.at[n], mrecv.at[k, q], m_ss.at[n], m_rs.at[k, q], target),
            send(bsend.at[n], brecv.at[k, q], b_ss.at[n], b_rs.at[k, q], target),
        )

    def pick(e, carry):
        sd, p, n = chip(e), core(e), e - 2
        srow = crow = jnp.zeros((1, 128), F32)
        for i in range(8):
            for m in range(4):
                t = idx_sm[sd, p * 4 + m, i]
                bsend[n, i * 4 + m] = b_vm[t]
                here = place == m * 8 + i
                srow = jnp.where(here, stable[pl.ds(t, 1), :] * as_sm[sd, p * 4 + m, i], srow)
                crow = jnp.where(here, ctable[pl.ds(t, 1), :], crow)
        msend[n, 0:1, :] = srow
        msend[n, 1:2, :] = crow * 8.0

        @pl.when((e > 2) & (e < 17))
        def _():
            for copy in to_peer(e - 1):
                copy.start()

        return carry

    lax.fori_loop(2, 18, pick, 0)
    for copy in to_peer(17):
        copy.start()
    own = [
        pltpu.make_async_copy(msend.at[14], mrecv.at[k, q], local_sem.at[8]),
        pltpu.make_async_copy(bsend.at[14], brecv.at[k, q], local_sem.at[9]),
    ]
    for copy in own:
        copy.start()

    send(other_half, arecv.at[k, 1 - q], a_ss.at[0], a_rs.at[0], dev(s, 1 - q, r)).wait_recv()
    for p in range(2):
        send(other_half, arecv.at[kx, p], a_ss.at[1 + p], a_rs.at[1 + p], dev(s, p, rx)).wait_recv()
    for h, dy in enumerate(HOPS):
        for j, slot in enumerate((k, kx)):
            n = 3 + 2 * h + j
            copy = send(arecv.at[slot], arecv.at[slot], a_ss.at[n], a_rs.at[n], dev(s, q, row_at(dy)))
            copy.start()
            a_sends.append(copy)
    for copy in own:
        copy.wait()

    group = lax.broadcasted_iota(I32, (8, 128), 1) // 32
    low, high = group % 2 == 0, group < 2
    quarter = lax.broadcasted_iota(I32, (32, 128), 1) // 32

    def out_copy(e):
        return pltpu.make_async_copy(xs.at[e % 2], xout.at[e], out_sem.at[e])

    def scales_copy(e):
        sb, p = chip_behind(e), core(e)
        return pltpu.make_async_copy(mrecv.at[(sb + r) % 8, p], m_sm.at[e], msm_sem.at[e])

    def finish(e):
        for i in range(8):
            for m in range(4):
                rows = [prods[e % 2, i, m * 32 + h * 8:m * 32 + h * 8 + 8, :] for h in range(4)]
                for n, block in enumerate(lane_groups(rows, low, high)):
                    w = m * 4 + n
                    xs[e % 2, i, w] = block * m_sm[e, 0, w * 8 + i]

    def process(e, carry, late=True):
        sb, p = chip_behind(e), core(e)
        kb = (sb + r) % 8
        source = dev(sb, p, r)

        @pl.when(e > 0)
        def _():
            send(msend.at[0], mrecv.at[kb, p], m_ss.at[0], m_rs.at[kb, p], source).wait_recv()

        scales_copy(e).start()
        ocols[pl.ds(e, 1), :] = mrecv[kb, p, 1:2, :].astype(I32)

        @pl.when(e == 2)
        def _():
            for h, dy in enumerate(HOPS):
                rb = row_at(4 - dy)
                for j, rr in enumerate((rb, (rb // 2) * 2 + (1 - xh))):
                    slot = (s + rr) % 8
                    n = 3 + 2 * h + j
                    send(arecv.at[slot], arecv.at[slot], a_ss.at[n], a_rs.at[n], dev(s, q, rb)).wait_recv()

        @pl.when(e > 0)
        def _():
            send(bsend.at[0], brecv.at[kb, p], b_ss.at[0], b_rs.at[kb, p], source).wait_recv()

        if late:
            scales_copy(e - 1).wait()

            @pl.when(e >= 3)
            def _():
                out_copy(e - 3).wait()

        if late:
            finish(e - 1)
        for i in range(8):
            a = arecv[kb, p, i]
            zero = jnp.zeros_like(a)
            left = jnp.concatenate([jnp.where(quarter == m, a, zero) for m in range(4)], axis=0)
            right = brecv[kb, p, i * 4:i * 4 + 4].reshape(128, 128)
            prods[e % 2, i] = jnp.dot(left, right, preferred_element_type=F32)
        if late:
            out_copy(e - 1).start()
        return carry

    process(0, 0, late=False)
    lax.fori_loop(1, 16, process, 0)
    scales_copy(15).wait()
    out_copy(13).wait()
    finish(15)
    out_copy(15).start()
    for copy in idx_sends + a_sends:
        copy.wait_send()
    for e in range(2, 18):
        if e != 16:
            for copy in to_peer(e):
                copy.wait_send()
    for e in (14, 15):
        out_copy(e).wait()


def scatter_kernel(cols, x_ref, out_ref, x, sem, *accs):
    g = pl.program_id(0)

    @pl.when(g == 0)
    def _():
        def load(e):
            return pltpu.make_async_copy(x_ref.at[e], x.at[e], sem.at[e])

        for e in range(16):
            load(e).start()

        def clear(t, _):
            for acc in accs:
                acc[pl.ds(pl.multiple_of(t * 64, 64), 64), :] = jnp.zeros((64, 128), F32)
            return _

        lax.fori_loop(0, 64, clear, 0)

        def add(e, _):
            load(e).wait()
            for w in range(16):
                at = [pl.ds(pl.multiple_of(cols[e, w * 8 + i], 8), 8) for i in range(8)]
                new = [acc[at[i], :] + x[e, i, w] for i, acc in enumerate(accs)]
                for i, acc in enumerate(accs):
                    acc[at[i], :] = new[i]
            return _

        lax.fori_loop(0, 16, add, 0)

    group = lax.broadcasted_iota(I32, (16, 128), 1) // 32
    low, high = group % 2 == 0, group < 2
    for i, acc in enumerate(accs):
        @pl.when(g == i)
        def _(acc=acc):
            def tile(t, _):
                for u in range(8):
                    base = pl.multiple_of((t * 8 + u) * 64, 64)
                    v = [
                        jnp.concatenate([acc[pl.ds(base + n * 8, 8), :], acc[pl.ds(base + 32 + n * 8, 8), :]], axis=0).astype(BF16)
                        for n in range(4)
                    ]
                    w = lane_groups(v, low, high)
                    for h in range(4):
                        lanes = pl.ds(pl.multiple_of((t * 8 + u) * 256, 256), 256)
                        out_ref[0, h * 8:h * 8 + 8, lanes] = jnp.concatenate([w[h][0:8], w[h][8:16]], axis=1)
                return _

            lax.fori_loop(0, 8, tile, 0)


def on_device(a_blocks, a_scale, a_cols, b_blocks, b_scale, b_cols):
    hbm = pl.BlockSpec(memory_space=pltpu.HBM)
    dma = pltpu.SemaphoreType.DMA
    x, cols = pl.pallas_call(
        exchange_kernel,
        name="exchange",
        out_shape=(
            jax.ShapeDtypeStruct((16, 8, 16, 8, 128), F32),
            jax.ShapeDtypeStruct((16, 128), I32),
        ),
        in_specs=[hbm] * 6,
        out_specs=(hbm, pl.BlockSpec(memory_space=pltpu.VMEM)),
        scratch_shapes=[
            pltpu.VMEM((512, 32, 128), BF16),
            pltpu.VMEM((16, 32, 128), BF16),
            pltpu.VMEM((4, 512), F32),
            pltpu.VMEM((4, 512), I32),
            pltpu.VMEM((4, 16), I32),
            pltpu.VMEM((4, 16), F32),
            pltpu.VMEM((16, 32, 32, 128), BF16),
            pltpu.VMEM((8, 2, 32, 32, 128), BF16),
            pltpu.VMEM((8, 2, 8, 32, 128), BF16),
            pltpu.VMEM((2, 8, 128, 128), F32),
            pltpu.VMEM((2, 8, 16, 8, 128), F32),
            pltpu.VMEM((8, 128), I32),
            pltpu.VMEM((8, 8, 128), I32),
            pltpu.VMEM((8, 128), F32),
            pltpu.VMEM((8, 8, 128), F32),
            pltpu.SMEM((8, 8, 128), I32),
            pltpu.SMEM((8, 8, 128), F32),
            pltpu.VMEM((512, 128), F32),
            pltpu.VMEM((512, 128), F32),
            pltpu.VMEM((16, 8, 128), F32),
            pltpu.VMEM((8, 2, 8, 128), F32),
            pltpu.SMEM((16, 8, 128), F32),
            dma((10,)), dma((16,)), dma((16,)), dma((7,)), dma((8,)), dma((7,)), dma((8,)),
            dma((16,)), dma((8, 2)), dma((16,)), dma((8, 2)), dma((9,)), dma((9,)),
        ],
        compiler_params=pltpu.CompilerParams(collective_id=0, has_side_effects=True, vmem_limit_bytes=67043328),
    )(a_cols[0, 0].T, a_scale[0, 0].T, a_blocks[0, 0], b_blocks[0, 0], b_scale[0, 0].T, b_cols[0, 0].T)
    out = pl.pallas_call(
        scatter_kernel,
        name="scatter",
        grid=(8,),
        out_shape=jax.ShapeDtypeStruct((8, 32, 16384), BF16),
        in_specs=[pl.BlockSpec(memory_space=pltpu.SMEM), hbm],
        out_specs=pl.BlockSpec((1, 32, 16384), lambda g: (g, 0, 0)),
        scratch_shapes=[pltpu.VMEM((16, 8, 16, 8, 128), F32), dma((16,))] + [pltpu.VMEM((4096, 128), F32)] * 8,
        compiler_params=pltpu.CompilerParams(vmem_limit_bytes=67043328),
    )(cols, x)
    return out[None, None]


def solution(mesh):
    blocks = P("col", "row", None, None, None)
    small = P("col", "row", None, None)
    return jax.shard_map(
        on_device,
        mesh=mesh,
        in_specs=(blocks, small, small, blocks, small, small),
        out_specs=blocks,
        check_vma=False,
    )
```

```python
import jax
import jax.numpy as jnp
from jax import lax
from jax.experimental import pallas as pl
from jax.experimental.pallas import tpu as pltpu
from jax.sharding import PartitionSpec as P

MESH = pl.DeviceIdType.MESH
F32, BF16, I32 = jnp.float32, jnp.bfloat16, jnp.int32

HOPS = (1, 3, 2)
CHIPS = (0, 7, 6, 3, 5, 2, 4, 1)


def lane_groups(v, low, high):
    t, w = [None] * 4, [None] * 4
    for i in (0, 2):
        turned = pltpu.roll(jnp.where(low, v[i + 1], v[i]), 32, 1)
        t[i], t[i + 1] = jnp.where(low, v[i], turned), jnp.where(low, turned, v[i + 1])
    for i in (0, 1):
        turned = pltpu.roll(jnp.where(high, t[i + 2], t[i]), 64, 1)
        w[i], w[i + 2] = jnp.where(high, t[i], turned), jnp.where(high, turned, t[i + 2])
    return [w[0], jnp.where(low, w[3], w[1]), w[2], jnp.where(low, w[1], w[3])]


def exchange_kernel(
    cols_ref, scale_ref, a_ref, b_ref, bs_ref, bc_ref,
    xout, ocols, z0, z1, z2, z3, z4, z5, z6, z7,
    b_vm, a_vm, bs_vm, bc_vm, cols_vm, scale_vm, bsend, brecv, arecv, prods,
    idx_s, idx_r, as_s, as_r, idx_sm, as_sm, ctable, stable, msend, mrecv, m_sm,
    local_sem, msm_sem, idx_ss, idx_rs, as_ss, as_rs, b_ss, b_rs, m_ss, m_rs, a_ss, a_rs,
):
    c, r = lax.axis_index("col"), lax.axis_index("row")
    s, q = c // 2, c % 2
    z, xl, y, xh = s // 2, s % 2, r // 2, r % 2
    k = (s + r) % 8
    rx = y * 2 + (1 - xh)
    kx = (s + rx) % 8

    def dev(s_, q_, r_):
        return {"row": r_, "col": 2 * s_ + q_}

    def hop(e):
        t = (e // 2) % 8
        f = t * 0
        for n, number in enumerate(CHIPS):
            f = jnp.where(t == n, number, f)
        dx, h = f % 2, f // 2
        return h + h // 2 - 2 * (h // 3), xl + dx - 2 * xl * dx

    def chip(e):
        dz, x = hop(e)
        return ((z + dz) % 4) * 2 + x

    def chip_behind(e):
        dz, x = hop(e)
        return ((z + 4 - dz) % 4) * 2 + x

    def core(e):
        return (q + e) % 2

    def row_at(dy):
        return ((y + dy) % 4) * 2 + xh

    def send(src, dst, ssem, rsem, target):
        return pltpu.make_async_remote_copy(
            src_ref=src, dst_ref=dst, send_sem=ssem, recv_sem=rsem, device_id=target, device_id_type=MESH
        )

    loads = [
        pltpu.make_async_copy(src, dst, local_sem.at[n])
        for n, (src, dst) in enumerate(
            ((cols_ref, cols_vm), (scale_ref, scale_vm), (a_ref, a_vm), (bs_ref, bs_vm), (bc_ref, bc_vm), (b_ref, b_vm))
        )
    ]
    for copy in loads:
        copy.start()

    barrier = pltpu.get_barrier_semaphore()
    peers = []
    for e in range(1, 8):
        peers.append(dev((s + 8 - e) % 8, q, (r + e) % 8))
    for e in range(1, 16):
        peers.append(dev(chip(e), core(e), r))
    for p in range(2):
        peers.append(dev(s, p, rx))
    for dy in HOPS:
        peers.append(dev(s, q, row_at(dy)))
    for peer in peers:
        pl.semaphore_signal(barrier, inc=1, device_id=peer, device_id_type=MESH)
    idx_s[...] = jnp.zeros_like(idx_s)
    as_s[...] = jnp.zeros_like(as_s)
    loads[0].wait()
    loads[1].wait()
    for p in range(2):
        idx_s[p * 4:p * 4 + 4, 0:8] = cols_vm[:, p * 8:p * 8 + 8]
        as_s[p * 4:p * 4 + 4, 0:8] = scale_vm[:, p * 8:p * 8 + 8]
    loads[2].wait()
    pl.semaphore_wait(barrier, len(peers))

    idx_sends = []
    for e in range(1, 8):
        to = dev((s + 8 - e) % 8, q, (r + e) % 8)
        idx_sends.append(send(idx_s, idx_r.at[s], idx_ss.at[e - 1], idx_rs.at[s], to))
        idx_sends.append(send(as_s, as_r.at[s], as_ss.at[e - 1], as_rs.at[s], to))
    for copy in idx_sends:
        copy.start()

    own_rows = pl.ds(pl.multiple_of(q * 8, 8), 8)
    other_half = a_vm.at[pl.ds(pl.multiple_of((1 - q) * 8, 8), 8)]
    a_sends = [send(a_vm.at[pl.ds(p * 8, 8)], arecv.at[k, q], a_ss.at[1 + p], a_rs.at[1 + q], dev(s, p, rx)) for p in range(2)]
    a_sends.append(send(other_half, arecv.at[k, q], a_ss.at[0], a_rs.at[0], dev(s, 1 - q, r)))
    for copy in a_sends:
        copy.start()
    arecv[k, q] = a_vm[own_rows]

    idx_r[s] = idx_s[...]
    as_r[s] = as_s[...]
    loads[3].wait()
    loads[4].wait()
    for g in range(4):
        lanes = pl.ds(g * 128, 128)
        for src, table in ((bs_vm, stable), (bc_vm, ctable)):
            v = src[:, lanes].astype(F32)
            eights = [jnp.broadcast_to(v[n:n + 1, :], (8, 128)) for n in range(4)]
            table[lanes, :] = jnp.transpose(jnp.concatenate(eights * 4, axis=0))

    def clear(t, carry):
        for acc in (z0, z1, z2, z3, z4, z5, z6, z7):
            acc[pl.ds(pl.multiple_of(t * 64, 64), 64), :] = jnp.zeros((64, 128), F32)
        return carry

    lax.fori_loop(0, 64, clear, 0)

    for e in range(1, 8):
        sb, rb = (s + e) % 8, (r + 8 - e) % 8
        send(idx_s, idx_r.at[sb], idx_ss.at[e - 1], idx_rs.at[sb], dev(sb, q, rb)).wait_recv()
        send(as_s, as_r.at[sb], as_ss.at[e - 1], as_rs.at[sb], dev(sb, q, rb)).wait_recv()
    to_smem = [pltpu.make_async_copy(idx_r, idx_sm, local_sem.at[6]), pltpu.make_async_copy(as_r, as_sm, local_sem.at[7])]
    for copy in to_smem:
        copy.start()
    for copy in to_smem:
        copy.wait()
    loads[5].wait()

    lane = lax.broadcasted_iota(I32, (1, 128), 1)
    place = lane // 32 * 8 + lane % 8

    def to_peer(e):
        target = dev(chip(e), core(e), r)
        n = e - 2
        return (
            send(msend.at[n], mrecv.at[k, q], m_ss.at[n], m_rs.at[k, q], target),
            send(bsend.at[n], brecv.at[k, q], b_ss.at[n], b_rs.at[k, q], target),
        )

    def pick(e, carry):
        sd, p, n = chip(e), core(e), e - 2
        srow = crow = jnp.zeros((1, 128), F32)
        for i in range(8):
            for m in range(4):
                t = idx_sm[sd, p * 4 + m, i]
                bsend[n, i * 4 + m] = b_vm[t]
                here = place == m * 8 + i
                srow = jnp.where(here, stable[pl.ds(t, 1), :] * as_sm[sd, p * 4 + m, i], srow)
                crow = jnp.where(here, ctable[pl.ds(t, 1), :], crow)
        msend[n, 0:1, :] = srow
        msend[n, 1:2, :] = crow * 8.0

        @pl.when((e > 2) & (e < 17))
        def _():
            for copy in to_peer(e - 1):
                copy.start()

        return carry

    lax.fori_loop(2, 18, pick, 0)
    for copy in to_peer(17):
        copy.start()
    own = [
        pltpu.make_async_copy(msend.at[14], mrecv.at[k, q], local_sem.at[8]),
        pltpu.make_async_copy(bsend.at[14], brecv.at[k, q], local_sem.at[9]),
    ]
    for copy in own:
        copy.start()

    send(other_half, arecv.at[k, 1 - q], a_ss.at[0], a_rs.at[0], dev(s, 1 - q, r)).wait_recv()
    for p in range(2):
        send(other_half, arecv.at[kx, p], a_ss.at[1 + p], a_rs.at[1 + p], dev(s, p, rx)).wait_recv()
    for h, dy in enumerate(HOPS):
        for j, slot in enumerate((k, kx)):
            n = 3 + 2 * h + j
            copy = send(arecv.at[slot], arecv.at[slot], a_ss.at[n], a_rs.at[n], dev(s, q, row_at(dy)))
            copy.start()
            a_sends.append(copy)
    for copy in own:
        copy.wait()

    group = lax.broadcasted_iota(I32, (8, 128), 1) // 32
    low, high = group % 2 == 0, group < 2
    quarter = lax.broadcasted_iota(I32, (32, 128), 1) // 32

    def scales_copy(e):
        sb, p = chip_behind(e), core(e)
        return pltpu.make_async_copy(mrecv.at[(sb + r) % 8, p], m_sm.at[e], msm_sem.at[e])

    def finish(e):
        for i in range(8):
            for m in range(4):
                rows = [prods[e % 2, i, m * 32 + h * 8:m * 32 + h * 8 + 8, :] for h in range(4)]
                for n, block in enumerate(lane_groups(rows, low, high)):
                    w = m * 4 + n
                    xout[e, i, w] = block * m_sm[e, 0, w * 8 + i]

    def process(e, carry, late=True):
        sb, p = chip_behind(e), core(e)
        kb = (sb + r) % 8
        source = dev(sb, p, r)

        @pl.when(e > 0)
        def _():
            send(msend.at[0], mrecv.at[kb, p], m_ss.at[0], m_rs.at[kb, p], source).wait_recv()

        scales_copy(e).start()
        ocols[pl.ds(e, 1), :] = mrecv[kb, p, 1:2, :].astype(I32)

        @pl.when(e == 2)
        def _():
            for h, dy in enumerate(HOPS):
                rb = row_at(4 - dy)
                for j, rr in enumerate((rb, (rb // 2) * 2 + (1 - xh))):
                    slot = (s + rr) % 8
                    n = 3 + 2 * h + j
                    send(arecv.at[slot], arecv.at[slot], a_ss.at[n], a_rs.at[n], dev(s, q, rb)).wait_recv()

        @pl.when(e > 0)
        def _():
            send(bsend.at[0], brecv.at[kb, p], b_ss.at[0], b_rs.at[kb, p], source).wait_recv()

        if late:
            scales_copy(e - 1).wait()

        if late:
            finish(e - 1)
        for i in range(8):
            a = arecv[kb, p, i]
            zero = jnp.zeros_like(a)
            left = jnp.concatenate([jnp.where(quarter == m, a, zero) for m in range(4)], axis=0)
            right = brecv[kb, p, i * 4:i * 4 + 4].reshape(128, 128)
            prods[e % 2, i] = jnp.dot(left, right, preferred_element_type=F32)
        return carry

    process(0, 0, late=False)
    lax.fori_loop(1, 16, process, 0)
    scales_copy(15).wait()
    finish(15)
    for copy in idx_sends + a_sends:
        copy.wait_send()
    for e in range(2, 18):
        if e != 16:
            for copy in to_peer(e):
                copy.wait_send()


def scatter_kernel(cols, x, *refs):
    out_ref, accs, tiles, sem = refs[8], refs[9:17], refs[17], refs[18]

    def add(e, _):
        for w in range(16):
            at = [pl.ds(pl.multiple_of(cols[e, w * 8 + i], 8), 8) for i in range(8)]
            new = [acc[at[i], :] + x[e, i, w] for i, acc in enumerate(accs)]
            for i, acc in enumerate(accs):
                acc[at[i], :] = new[i]
        return _

    lax.fori_loop(0, 16, add, 0)

    group = lax.broadcasted_iota(I32, (16, 128), 1) // 32
    low, high = group % 2 == 0, group < 2

    def out_copy(i, t):
        lanes = pl.ds(pl.multiple_of(t * 2048, 2048), 2048)
        return pltpu.make_async_copy(tiles.at[i, :, lanes], out_ref.at[i, :, lanes], sem.at[i, t])

    for i, acc in enumerate(accs):
        def tile(t, _):
            for u in range(8):
                base = pl.multiple_of((t * 8 + u) * 64, 64)
                v = [
                    jnp.concatenate([acc[pl.ds(base + n * 8, 8), :], acc[pl.ds(base + 32 + n * 8, 8), :]], axis=0).astype(BF16)
                    for n in range(4)
                ]
                w = lane_groups(v, low, high)
                for h in range(4):
                    lanes = pl.ds(pl.multiple_of((t * 8 + u) * 256, 256), 256)
                    tiles[i, h * 8:h * 8 + 8, lanes] = jnp.concatenate([w[h][0:8], w[h][8:16]], axis=1)
            out_copy(i, t).start()
            return _

        lax.fori_loop(0, 8, tile, 0)
    for i in range(8):
        for t in range(8):
            out_copy(i, t).wait()


def on_device(a_blocks, a_scale, a_cols, b_blocks, b_scale, b_cols):
    hbm = pl.BlockSpec(memory_space=pltpu.HBM)
    vmem = pl.BlockSpec(memory_space=pltpu.VMEM)
    dma = pltpu.SemaphoreType.DMA
    sums = jax.ShapeDtypeStruct((4096, 128), F32)
    x, cols, *zeros = pl.pallas_call(
        exchange_kernel,
        name="exchange",
        out_shape=(
            jax.ShapeDtypeStruct((16, 8, 16, 8, 128), F32),
            jax.ShapeDtypeStruct((16, 128), I32),
        ) + (sums,) * 8,
        in_specs=[hbm] * 6,
        out_specs=(vmem,) * 10,
        scratch_shapes=[
            pltpu.VMEM((512, 32, 128), BF16),
            pltpu.VMEM((16, 32, 128), BF16),
            pltpu.VMEM((4, 512), F32),
            pltpu.VMEM((4, 512), I32),
            pltpu.VMEM((4, 16), I32),
            pltpu.VMEM((4, 16), F32),
            pltpu.VMEM((16, 32, 32, 128), BF16),
            pltpu.VMEM((8, 2, 32, 32, 128), BF16),
            pltpu.VMEM((8, 2, 8, 32, 128), BF16),
            pltpu.VMEM((2, 8, 128, 128), F32),
            pltpu.VMEM((8, 128), I32),
            pltpu.VMEM((8, 8, 128), I32),
            pltpu.VMEM((8, 128), F32),
            pltpu.VMEM((8, 8, 128), F32),
            pltpu.SMEM((8, 8, 128), I32),
            pltpu.SMEM((8, 8, 128), F32),
            pltpu.VMEM((512, 128), F32),
            pltpu.VMEM((512, 128), F32),
            pltpu.VMEM((16, 8, 128), F32),
            pltpu.VMEM((8, 2, 8, 128), F32),
            pltpu.SMEM((16, 8, 128), F32),
            dma((10,)), dma((16,)), dma((7,)), dma((8,)), dma((7,)), dma((8,)),
            dma((16,)), dma((8, 2)), dma((16,)), dma((8, 2)), dma((9,)), dma((9,)),
        ],
        compiler_params=pltpu.CompilerParams(collective_id=0, has_side_effects=True, vmem_limit_bytes=24 << 20),
    )(*[pltpu.with_memory_space_constraint(v, pltpu.HBM) for v in (a_cols[0, 0].T, a_scale[0, 0].T, a_blocks[0, 0], b_blocks[0, 0], b_scale[0, 0].T, b_cols[0, 0].T)])
    out, *_ = pl.pallas_call(
        scatter_kernel,
        name="scatter",
        out_shape=(jax.ShapeDtypeStruct((8, 32, 16384), BF16),) + (sums,) * 8,
        input_output_aliases={n + 2: n + 1 for n in range(8)},
        in_specs=[pl.BlockSpec(memory_space=pltpu.SMEM)] + [vmem] * 9,
        out_specs=(hbm,) + (vmem,) * 8,
        scratch_shapes=[pltpu.VMEM((8, 32, 16384), BF16), dma((8, 8))],
        compiler_params=pltpu.CompilerParams(vmem_limit_bytes=24 << 20),
    )(cols, x, *zeros)
    return out[None, None]


def solution(mesh):
    blocks = P("col", "row", None, None, None)
    small = P("col", "row", None, None)
    return jax.shard_map(
        on_device,
        mesh=mesh,
        in_specs=(blocks, small, small, blocks, small, small),
        out_specs=blocks,
        check_vma=False,
    )
```

```python
import jax
import jax.numpy as jnp
from jax import lax
from jax.experimental import pallas as pl
from jax.experimental.pallas import tpu as pltpu
from jax.sharding import PartitionSpec as P

MESH = pl.DeviceIdType.MESH
F32, BF16, I32 = jnp.float32, jnp.bfloat16, jnp.int32

HOPS = (1, 3, 2)
CHIPS = (0, 7, 6, 3, 5, 2, 4, 1)


def lane_groups(v, low, high):
    t, w = [None] * 4, [None] * 4
    for i in (0, 2):
        turned = pltpu.roll(jnp.where(low, v[i + 1], v[i]), 32, 1)
        t[i], t[i + 1] = jnp.where(low, v[i], turned), jnp.where(low, turned, v[i + 1])
    for i in (0, 1):
        turned = pltpu.roll(jnp.where(high, t[i + 2], t[i]), 64, 1)
        w[i], w[i + 2] = jnp.where(high, t[i], turned), jnp.where(high, turned, t[i + 2])
    return [w[0], jnp.where(low, w[3], w[1]), w[2], jnp.where(low, w[1], w[3])]


def exchange_kernel(
    cols_ref, scale_ref, a_ref, b_ref, bs_ref, bc_ref,
    xout, ocols, z0, z1, z2, z3, z4, z5, z6, z7,
    b_vm, a_vm, bs_vm, bc_vm, cols_vm, scale_vm, bsend, brecv, arecv, prods,
    idx_s, idx_r, as_s, as_r, idx_sm, as_sm, ctable, stable, msend, mrecv, m_sm,
    local_sem, msm_sem, idx_ss, idx_rs, as_ss, as_rs, b_ss, b_rs, m_ss, m_rs, a_ss, a_rs,
):
    c, r = lax.axis_index("col"), lax.axis_index("row")
    s, q = c // 2, c % 2
    z, xl, y, xh = s // 2, s % 2, r // 2, r % 2
    k = (s + r) % 8
    rx = y * 2 + (1 - xh)
    kx = (s + rx) % 8

    def dev(s_, q_, r_):
        return {"row": r_, "col": 2 * s_ + q_}

    def hop(e):
        t = (e // 2) % 8
        f = t * 0
        for n, number in enumerate(CHIPS):
            f = jnp.where(t == n, number, f)
        dx, h = f % 2, f // 2
        return h + h // 2 - 2 * (h // 3), xl + dx - 2 * xl * dx

    def chip(e):
        dz, x = hop(e)
        return ((z + dz) % 4) * 2 + x

    def chip_behind(e):
        dz, x = hop(e)
        return ((z + 4 - dz) % 4) * 2 + x

    def core(e):
        return (q + e) % 2

    def row_at(dy):
        return ((y + dy) % 4) * 2 + xh

    def send(src, dst, ssem, rsem, target):
        return pltpu.make_async_remote_copy(
            src_ref=src, dst_ref=dst, send_sem=ssem, recv_sem=rsem, device_id=target, device_id_type=MESH
        )

    loads = [
        pltpu.make_async_copy(src, dst, local_sem.at[n])
        for n, (src, dst) in enumerate(
            ((cols_ref, cols_vm), (scale_ref, scale_vm), (a_ref, a_vm), (bs_ref, bs_vm), (bc_ref, bc_vm), (b_ref, b_vm))
        )
    ]
    for copy in loads:
        copy.start()

    barrier = pltpu.get_barrier_semaphore()
    def greet(peer):
        pl.semaphore_signal(barrier, inc=1, device_id=peer, device_id_type=MESH)

    def greet_diagonal(e, carry):
        greet(dev((s + 8 - e) % 8, q, (r + e) % 8))
        return carry

    def greet_column(e, carry):
        greet(dev(chip(e), core(e), r))
        return carry

    lax.fori_loop(1, 8, greet_diagonal, 0)
    lax.fori_loop(1, 16, greet_column, 0)
    for p in range(2):
        greet(dev(s, p, rx))
    for dy in HOPS:
        greet(dev(s, q, row_at(dy)))
    idx_s[...] = jnp.zeros_like(idx_s)
    as_s[...] = jnp.zeros_like(as_s)
    loads[0].wait()
    loads[1].wait()
    for p in range(2):
        idx_s[p * 4:p * 4 + 4, 0:8] = cols_vm[:, p * 8:p * 8 + 8]
        as_s[p * 4:p * 4 + 4, 0:8] = scale_vm[:, p * 8:p * 8 + 8]
    loads[2].wait()
    pl.semaphore_wait(barrier, 27)

    idx_sends = []
    for e in range(1, 8):
        to = dev((s + 8 - e) % 8, q, (r + e) % 8)
        idx_sends.append(send(idx_s, idx_r.at[s], idx_ss.at[e - 1], idx_rs.at[s], to))
        idx_sends.append(send(as_s, as_r.at[s], as_ss.at[e - 1], as_rs.at[s], to))
    for copy in idx_sends:
        copy.start()

    own_rows = pl.ds(pl.multiple_of(q * 8, 8), 8)
    other_half = a_vm.at[pl.ds(pl.multiple_of((1 - q) * 8, 8), 8)]
    a_sends = [send(a_vm.at[pl.ds(p * 8, 8)], arecv.at[k, q], a_ss.at[1 + p], a_rs.at[1 + q], dev(s, p, rx)) for p in range(2)]
    a_sends.append(send(other_half, arecv.at[k, q], a_ss.at[0], a_rs.at[0], dev(s, 1 - q, r)))
    for copy in a_sends:
        copy.start()
    arecv[k, q] = a_vm[own_rows]

    idx_r[s] = idx_s[...]
    as_r[s] = as_s[...]
    loads[3].wait()
    loads[4].wait()
    for g in range(4):
        lanes = pl.ds(g * 128, 128)
        for src, table in ((bs_vm, stable), (bc_vm, ctable)):
            v = src[:, lanes].astype(F32)
            eights = [jnp.broadcast_to(v[n:n + 1, :], (8, 128)) for n in range(4)]
            table[lanes, :] = jnp.transpose(jnp.concatenate(eights * 4, axis=0))

    def clear(t, carry):
        for acc in (z0, z1, z2, z3, z4, z5, z6, z7):
            acc[pl.ds(pl.multiple_of(t * 64, 64), 64), :] = jnp.zeros((64, 128), F32)
        return carry

    lax.fori_loop(0, 64, clear, 0)

    for e in range(1, 8):
        sb, rb = (s + e) % 8, (r + 8 - e) % 8
        send(idx_s, idx_r.at[sb], idx_ss.at[e - 1], idx_rs.at[sb], dev(sb, q, rb)).wait_recv()
        send(as_s, as_r.at[sb], as_ss.at[e - 1], as_rs.at[sb], dev(sb, q, rb)).wait_recv()
    to_smem = [pltpu.make_async_copy(idx_r, idx_sm, local_sem.at[6]), pltpu.make_async_copy(as_r, as_sm, local_sem.at[7])]
    for copy in to_smem:
        copy.start()
    for copy in to_smem:
        copy.wait()
    loads[5].wait()

    lane = lax.broadcasted_iota(I32, (1, 128), 1)
    place = lane // 32 * 8 + lane % 8

    def to_peer(e):
        target = dev(chip(e), core(e), r)
        n = e - 2
        return (
            send(msend.at[n], mrecv.at[k, q], m_ss.at[n], m_rs.at[k, q], target),
            send(bsend.at[n], brecv.at[k, q], b_ss.at[n], b_rs.at[k, q], target),
        )

    def pick(e, carry):
        sd, p, n = chip(e), core(e), e - 2
        srow = crow = jnp.zeros((1, 128), F32)
        for i in range(8):
            for m in range(4):
                t = idx_sm[sd, p * 4 + m, i]
                bsend[n, i * 4 + m] = b_vm[t]
                here = place == m * 8 + i
                srow = jnp.where(here, stable[pl.ds(t, 1), :] * as_sm[sd, p * 4 + m, i], srow)
                crow = jnp.where(here, ctable[pl.ds(t, 1), :], crow)
        msend[n, 0:1, :] = srow
        msend[n, 1:2, :] = crow * 8.0

        @pl.when((e > 2) & (e < 17))
        def _():
            for copy in to_peer(e - 1):
                copy.start()

        return carry

    lax.fori_loop(2, 18, pick, 0)
    for copy in to_peer(17):
        copy.start()
    own = [
        pltpu.make_async_copy(msend.at[14], mrecv.at[k, q], local_sem.at[8]),
        pltpu.make_async_copy(bsend.at[14], brecv.at[k, q], local_sem.at[9]),
    ]
    for copy in own:
        copy.start()

    send(other_half, arecv.at[k, 1 - q], a_ss.at[0], a_rs.at[0], dev(s, 1 - q, r)).wait_recv()
    for p in range(2):
        send(other_half, arecv.at[kx, p], a_ss.at[1 + p], a_rs.at[1 + p], dev(s, p, rx)).wait_recv()
    for h, dy in enumerate(HOPS):
        for j, slot in enumerate((k, kx)):
            n = 3 + 2 * h + j
            copy = send(arecv.at[slot], arecv.at[slot], a_ss.at[n], a_rs.at[n], dev(s, q, row_at(dy)))
            copy.start()
            a_sends.append(copy)
    for copy in own:
        copy.wait()

    group = lax.broadcasted_iota(I32, (8, 128), 1) // 32
    low, high = group % 2 == 0, group < 2
    quarter = lax.broadcasted_iota(I32, (32, 128), 1) // 32

    def scales_copy(e):
        sb, p = chip_behind(e), core(e)
        return pltpu.make_async_copy(mrecv.at[(sb + r) % 8, p], m_sm.at[e], msm_sem.at[e])

    def finish(e):
        for i in range(8):
            for m in range(4):
                rows = [prods[e % 2, i, m * 32 + h * 8:m * 32 + h * 8 + 8, :] for h in range(4)]
                for n, block in enumerate(lane_groups(rows, low, high)):
                    w = m * 4 + n
                    xout[e, i, w] = block * m_sm[e, 0, w * 8 + i]

    def process(e, carry, late=True):
        sb, p = chip_behind(e), core(e)
        kb = (sb + r) % 8
        source = dev(sb, p, r)

        @pl.when(e > 0)
        def _():
            send(msend.at[0], mrecv.at[kb, p], m_ss.at[0], m_rs.at[kb, p], source).wait_recv()

        scales_copy(e).start()
        ocols[pl.ds(e, 1), :] = mrecv[kb, p, 1:2, :].astype(I32)

        @pl.when(e == 2)
        def _():
            for h, dy in enumerate(HOPS):
                rb = row_at(4 - dy)
                for j, rr in enumerate((rb, (rb // 2) * 2 + (1 - xh))):
                    slot = (s + rr) % 8
                    n = 3 + 2 * h + j
                    send(arecv.at[slot], arecv.at[slot], a_ss.at[n], a_rs.at[n], dev(s, q, rb)).wait_recv()

        @pl.when(e > 0)
        def _():
            send(bsend.at[0], brecv.at[kb, p], b_ss.at[0], b_rs.at[kb, p], source).wait_recv()

        if late:
            scales_copy(e - 1).wait()

        if late:
            finish(e - 1)
        for i in range(8):
            a = arecv[kb, p, i]
            zero = jnp.zeros_like(a)
            left = jnp.concatenate([jnp.where(quarter == m, a, zero) for m in range(4)], axis=0)
            right = brecv[kb, p, i * 4:i * 4 + 4].reshape(128, 128)
            prods[e % 2, i] = jnp.dot(left, right, preferred_element_type=F32)
        return carry

    process(0, 0, late=False)
    lax.fori_loop(1, 16, process, 0)
    scales_copy(15).wait()
    finish(15)
    for copy in idx_sends + a_sends:
        copy.wait_send()
    for e in range(2, 18):
        if e != 16:
            for copy in to_peer(e):
                copy.wait_send()


def scatter_kernel(cols, x, *refs):
    out_ref, accs, tiles, sem = refs[8], refs[9:17], refs[17], refs[18]

    def add(e, _):
        for w in range(16):
            at = [pl.ds(pl.multiple_of(cols[e, w * 8 + i], 8), 8) for i in range(8)]
            new = [acc[at[i], :] + x[e, i, w] for i, acc in enumerate(accs)]
            for i, acc in enumerate(accs):
                acc[at[i], :] = new[i]
        return _

    lax.fori_loop(0, 16, add, 0)

    group = lax.broadcasted_iota(I32, (16, 128), 1) // 32
    low, high = group % 2 == 0, group < 2

    def out_copy(i, t):
        lanes = pl.ds(pl.multiple_of(t * 2048, 2048), 2048)
        return pltpu.make_async_copy(tiles.at[i, :, lanes], out_ref.at[i, :, lanes], sem.at[i, t])

    for i, acc in enumerate(accs):
        def tile(t, _):
            for u in range(8):
                base = pl.multiple_of((t * 8 + u) * 64, 64)
                v = [
                    jnp.concatenate([acc[pl.ds(base + n * 8, 8), :], acc[pl.ds(base + 32 + n * 8, 8), :]], axis=0).astype(BF16)
                    for n in range(4)
                ]
                w = lane_groups(v, low, high)
                for h in range(4):
                    lanes = pl.ds(pl.multiple_of((t * 8 + u) * 256, 256), 256)
                    tiles[i, h * 8:h * 8 + 8, lanes] = jnp.concatenate([w[h][0:8], w[h][8:16]], axis=1)
            out_copy(i, t).start()
            return _

        lax.fori_loop(0, 8, tile, 0)
    for i in range(8):
        for t in range(8):
            out_copy(i, t).wait()


def on_device(a_blocks, a_scale, a_cols, b_blocks, b_scale, b_cols):
    hbm = pl.BlockSpec(memory_space=pltpu.HBM)
    vmem = pl.BlockSpec(memory_space=pltpu.VMEM)
    dma = pltpu.SemaphoreType.DMA
    sums = jax.ShapeDtypeStruct((4096, 128), F32)
    x, cols, *zeros = pl.pallas_call(
        exchange_kernel,
        name="exchange",
        out_shape=(
            jax.ShapeDtypeStruct((16, 8, 16, 8, 128), F32),
            jax.ShapeDtypeStruct((16, 128), I32),
        ) + (sums,) * 8,
        in_specs=[hbm] * 6,
        out_specs=(vmem,) * 10,
        scratch_shapes=[
            pltpu.VMEM((512, 32, 128), BF16),
            pltpu.VMEM((16, 32, 128), BF16),
            pltpu.VMEM((4, 512), F32),
            pltpu.VMEM((4, 512), I32),
            pltpu.VMEM((4, 16), I32),
            pltpu.VMEM((4, 16), F32),
            pltpu.VMEM((16, 32, 32, 128), BF16),
            pltpu.VMEM((8, 2, 32, 32, 128), BF16),
            pltpu.VMEM((8, 2, 8, 32, 128), BF16),
            pltpu.VMEM((2, 8, 128, 128), F32),
            pltpu.VMEM((8, 128), I32),
            pltpu.VMEM((8, 8, 128), I32),
            pltpu.VMEM((8, 128), F32),
            pltpu.VMEM((8, 8, 128), F32),
            pltpu.SMEM((8, 8, 128), I32),
            pltpu.SMEM((8, 8, 128), F32),
            pltpu.VMEM((512, 128), F32),
            pltpu.VMEM((512, 128), F32),
            pltpu.VMEM((16, 8, 128), F32),
            pltpu.VMEM((8, 2, 8, 128), F32),
            pltpu.SMEM((16, 8, 128), F32),
            dma((10,)), dma((16,)), dma((7,)), dma((8,)), dma((7,)), dma((8,)),
            dma((16,)), dma((8, 2)), dma((16,)), dma((8, 2)), dma((9,)), dma((9,)),
        ],
        compiler_params=pltpu.CompilerParams(collective_id=0, has_side_effects=True, vmem_limit_bytes=24 << 20),
    )(*[pltpu.with_memory_space_constraint(v, pltpu.HBM) for v in (a_cols[0, 0].T, a_scale[0, 0].T, a_blocks[0, 0], b_blocks[0, 0], b_scale[0, 0].T, b_cols[0, 0].T)])
    out, *_ = pl.pallas_call(
        scatter_kernel,
        name="scatter",
        out_shape=(jax.ShapeDtypeStruct((8, 32, 16384), BF16),) + (sums,) * 8,
        input_output_aliases={n + 2: n + 1 for n in range(8)},
        in_specs=[pl.BlockSpec(memory_space=pltpu.SMEM)] + [vmem] * 9,
        out_specs=(hbm,) + (vmem,) * 8,
        scratch_shapes=[pltpu.VMEM((8, 32, 16384), BF16), dma((8, 8))],
        compiler_params=pltpu.CompilerParams(vmem_limit_bytes=24 << 20),
    )(cols, x, *zeros)
    return out[None, None]


def solution(mesh):
    blocks = P("col", "row", None, None, None)
    small = P("col", "row", None, None)
    return jax.shard_map(
        on_device,
        mesh=mesh,
        in_specs=(blocks, small, small, blocks, small, small),
        out_specs=blocks,
        check_vma=False,
    )
```
